32 devices in a mesh: dp: 8 (over y, x, core), mp: 4 (over z).
Axes of the slice: x: 2, y: 2, z: 4, core: 2. Of those that a mesh axis runs over, the one named last changes fastest.
Arguments:
- patches: bfloat16 [1024, 6144], P('dp', 'mp'), may hold values from -64 to 64
- send_start: int32 [8, 8], P('dp'), may hold values from 0 to 128, as said below
- run_length: int32 [8, 8], P('dp'), may hold values from 0 to 32, as said below
- slot_start: int32 [8, 8], P('dp'), may hold values from 0 to 128, as said below
- image_ids: int32 [8, 128], P('dp'), may hold values from 0 to 7, never falling along the last dimension, each value on 1 to 32 neighbouring positions
- norm_gain: float32 [6144], replicated, may hold values from 0.1 to 1.9
- qkv_weight: bfloat16 [6144, 3, 4096], P('dp', None, 'mp'), may hold values from -0.078125 to 0.078125
- query_gain: float32 [128], replicated, may hold values from 0.1 to 1.9
- key_gain: float32 [128], replicated, may hold values from 0.1 to 1.9
- out_weight: bfloat16 [4096, 6144], P('mp'), may hold values from -0.09375 to 0.09375
Outputs:
- packed: bfloat16 [1024, 6144], P('dp', 'mp')
- attended: bfloat16 [1024, 6144], P('dp', 'mp')
The draws below stay inside these ranges and needn't reach their ends.
Inputs may be any that keep to these rules, and one draw needn't show every extreme that they name: `run_length`: every source's runs sum to 128 and every pack's runs sum to 128; the longest run is exactly 32. `send_start`: the runs of one source device do not intersect and cover its 128 rows. `slot_start`: the runs into one pack do not intersect and fill its 128 slots. `image_ids`: image numbers never fall along a pack; equal numbers mark one image.
All inputs are finite; a program needn't handle non-finite values.
Results may differ from the reference program's by a relative error of at most 0.011.
Values may be sent and summed in bfloat16 or wider, within the bound.
A program may use at most 128 MiB of HBM per device.

```python
import math
import jax
import jax.numpy as jnp
import numpy as np
from jax import lax

D = 6144
HEADS = 32
HS = 128
PACK = 128
PACKS = 8
TOKENS = 1024
CAP = 32
IMAGES = 8
IMG_MOST = 32
N_MP = 4


def ordered_starts(key_order, run_table):
    row_count = run_table.shape[0]
    rank_draw = jax.vmap(lambda subkey: jax.random.permutation(subkey, row_count))(jax.random.split(key_order, row_count)).astype(jnp.int32)
    sort_key = jnp.where(run_table == 0, rank_draw + row_count, rank_draw)
    visit_order = jnp.argsort(sort_key, axis=1, stable=True).astype(jnp.int32)
    ordered = jnp.take_along_axis(run_table, visit_order, axis=1)
    starts = jnp.cumsum(ordered, axis=1) - ordered
    position = jnp.argsort(visit_order, axis=1, stable=True).astype(jnp.int32)
    return jnp.take_along_axis(starts, position, axis=1).astype(jnp.int32)


def pack_plan(key):
    mean_run = PACK // PACKS
    half_count = PACKS // 2
    excess = jax.random.randint(jax.random.fold_in(key, 11), (half_count,), -mean_run, mean_run + 1).astype(jnp.int32)
    excess = excess.at[0].set(mean_run)
    profile = jnp.concatenate([mean_run + excess, mean_run - excess]).astype(jnp.int32)
    pack_perm = jax.random.permutation(jax.random.fold_in(key, 12), PACKS).astype(jnp.int32)
    source_perm = jax.random.permutation(jax.random.fold_in(key, 13), PACKS).astype(jnp.int32)
    run_table = profile[(source_perm[:, None] + pack_perm[None, :]) % PACKS]
    send_table = ordered_starts(jax.random.fold_in(key, 14), run_table)
    slot_table = ordered_starts(jax.random.fold_in(key, 15), jnp.transpose(run_table))
    return (send_table, run_table.astype(jnp.int32), slot_table)


def draw_send_start(key, part):
    return pack_plan(key)[0]


def draw_run_length(key, part):
    return pack_plan(key)[1]


def draw_slot_start(key, part):
    return pack_plan(key)[2]


def draw_patches(key, part):
    row_scale = jnp.exp(jax.random.uniform(jax.random.fold_in(key, 21), (TOKENS, 1), minval=-1.15, maxval=1.15))
    base = jnp.clip(jax.random.normal(jax.random.fold_in(key, 22), (TOKENS, D)), -6.0, 6.0)
    column_scale = jnp.exp(jax.random.uniform(jax.random.fold_in(key, 23), (1, D), minval=-1.15, maxval=1.15))
    return (base * row_scale * column_scale).astype(jnp.bfloat16)


def block_levels(rng, extent, cuts, smallest, top_value):
    gain = 1.0
    for dim, parts in cuts:
        heights = jax.random.uniform(jax.random.fold_in(jax.random.fold_in(rng, 6), dim), (parts,), jnp.float32, smallest / len(cuts), top_value / len(cuts))
        gain = gain * jnp.repeat(jnp.exp(heights), extent[dim] // parts).reshape((-1,) + (1,) * (len(extent) - 1 - dim))
    return gain


def split_up(count, total, most, skew):
    loads = [(1 << 20) // math.isqrt(standing ** skew) + 1 for standing in range(2, count + 1)]
    spare, holding = total - most - (count - 1), [1] * (count - 1)
    while spare > 0:
        candidates = [i for i in range(count - 1) if holding[i] < most]
        whole, budget = sum([loads[i] for i in candidates]), spare
        for i in candidates:
            more = min(most - holding[i], max(1, budget * loads[i] // whole), spare)
            holding[i] = holding[i] + more
            spare = spare - more
    return np.array([most] + holding)


def uneven(rng, amount, total, bound, lean):
    if amount == 2:
        one = jax.random.randint(rng, (), max(1, total - bound), min(bound, total - 1) + 1)
        return jnp.stack([one, total - one])
    tallies = jnp.asarray(split_up(amount, total, bound, lean), jnp.int32)
    couples = (amount - 1) // 2
    giver, taker = tallies[1:1 + 2 * couples:2], tallies[2:2 + 2 * couples:2]
    slack = jnp.minimum(giver - 1, bound - taker)
    shifted = jax.random.randint(jax.random.fold_in(rng, 1), (couples,), 0, 1 << 20) % (slack + 1)
    tallies = tallies.at[1:1 + 2 * couples:2].set(giver - shifted).at[2:2 + 2 * couples:2].set(taker + shifted)
    return tallies[jax.random.permutation(jax.random.fold_in(rng, 2), amount)]


def centred(key, shape, deviation, most, pieces=(), kind=jnp.bfloat16):
    loudness = block_levels(key, shape, pieces, -0.22, 0.18) if pieces else 1.0
    array = jax.random.normal(key, shape, jnp.float32) * deviation * loudness
    return jnp.minimum(jnp.maximum(array, -most), most).astype(kind)


def setup_inputs(seed: int = 0) -> dict:
    key_list = jax.random.split(jax.random.key(seed), 11)
    patches = draw_patches(jax.random.fold_in(key_list[10], 71), 0)
    send_start = draw_send_start(jax.random.fold_in(key_list[10], 71), 0)
    run_length = draw_run_length(jax.random.fold_in(key_list[10], 71), 0)
    slot_start = draw_slot_start(jax.random.fold_in(key_list[10], 71), 0)
    image_ids = jax.vmap(lambda own: jnp.searchsorted(jnp.cumsum(uneven(own, IMAGES, PACK, IMG_MOST, 2)), jnp.arange(PACK), side="right"))(jax.random.split(key_list[4], PACKS)).reshape((PACKS, PACK)).astype(jnp.int32)
    norm_gain = jnp.clip(1.0 + 0.18 * jax.random.normal(key_list[5], (D,), jnp.float32), 0.1, 1.9)
    qkv_weight = centred(key_list[6], (D, 3, HEADS * HS), D ** -0.5, 0.078125, ((0, 8), (2, 4)))
    query_gain = jnp.clip(1.0 + 0.18 * jax.random.normal(key_list[7], (HS,), jnp.float32), 0.1, 1.9)
    key_gain = jnp.clip(1.0 + 0.18 * jax.random.normal(key_list[8], (HS,), jnp.float32), 0.1, 1.9)
    out_weight = centred(key_list[9], (HEADS * HS, D), (HEADS * HS) ** -0.5, 0.09375, ((0, 4),))
    return dict(patches=patches, send_start=send_start, run_length=run_length, slot_start=slot_start, image_ids=image_ids, norm_gain=norm_gain, qkv_weight=qkv_weight, query_gain=query_gain, key_gain=key_gain, out_weight=out_weight)


epsilon = 1e-06

def row_norm(values, scales):
    middle = lax.optimization_barrier(jnp.mean(values, axis=-1, keepdims=True))
    spread = lax.optimization_barrier(jnp.mean(values * values, axis=-1, keepdims=True)) - middle * middle
    return (values - middle) * lax.rsqrt(spread + epsilon) * scales

def reference(patches, send_start, run_length, slot_start, image_ids, norm_gain, qkv_weight, query_gain, key_gain, out_weight):
    source = jnp.arange(PACKS, dtype=jnp.int32)[:, None, None]
    target = jnp.arange(PACKS, dtype=jnp.int32)[None, :, None]
    within = jnp.arange(CAP, dtype=jnp.int32)[None, None, :]
    source_rows = jnp.clip(source * PACK + send_start[:, :, None] + within, 0, TOKENS - 1)
    dest_rows = target * PACK + jnp.transpose(slot_start)[:, :, None] + within
    dest_rows = jnp.where(within < run_length[:, :, None], dest_rows, TOKENS)
    packed = jnp.zeros_like(patches).at[dest_rows.reshape(-1)].set(patches[source_rows.reshape(-1)], mode='drop')
    flat_weight = qkv_weight.reshape(D, 3 * HEADS * HS)
    out_groups = out_weight.astype(jnp.float32).reshape(N_MP, HEADS * HS // N_MP, D)

    def one_pack(inputs):
        pack_rows, image_of = inputs
        normed = row_norm(pack_rows.astype(jnp.float32), norm_gain).astype(jnp.bfloat16)
        projected = jnp.dot(normed, flat_weight, preferred_element_type=jnp.float32).reshape(PACK, 3, HEADS, HS)
        queries = row_norm(projected[:, 0], query_gain).astype(jnp.bfloat16)
        key_rows = row_norm(projected[:, 1], key_gain).astype(jnp.bfloat16)
        values = projected[:, 2].astype(jnp.bfloat16)
        scores = jnp.einsum('qhd,khd->hqk', queries.astype(jnp.float32), key_rows.astype(jnp.float32)) * HS ** (-0.5)
        same_image = image_of[:, None] == image_of[None, :]
        weights_raw = jnp.where(same_image[None], jnp.exp(scores), 0.0)
        totals = lax.optimization_barrier(jnp.sum(weights_raw, axis=-1, keepdims=True))
        attention = (weights_raw / totals).astype(jnp.bfloat16)
        context = jnp.einsum('hqk,khd->qhd', attention.astype(jnp.float32), values.astype(jnp.float32)).astype(jnp.bfloat16)
        grouped = context.reshape(PACK, N_MP, HEADS * HS // N_MP).astype(jnp.float32)
        group_terms = jnp.einsum('rgk,gkd->rgd', grouped, out_groups).astype(jnp.bfloat16)
        group_terms = lax.optimization_barrier(group_terms).astype(jnp.float32)
        return lax.optimization_barrier(jnp.sum(group_terms, axis=1)).astype(jnp.bfloat16)
    attended = lax.map(one_pack, (packed.reshape(PACKS, PACK, D), image_ids)).reshape(TOKENS, D)
    return (packed, attended)
```

```python
import functools

import jax
import jax.numpy as jnp
from jax import lax
from jax.experimental import pallas as pl
from jax.experimental.pallas import tpu as pltpu
from jax.sharding import PartitionSpec as P

MESH = pl.DeviceIdType.MESH
F32, BF16, I32 = jnp.float32, jnp.bfloat16, jnp.int32
epsilon = 1e-06


def row_norm(values, scales):
    middle = jnp.mean(values, axis=-1, keepdims=True)
    spread = jnp.mean(values * values, axis=-1, keepdims=True) - middle * middle
    return (values - middle) * lax.rsqrt(spread + epsilon) * scales


def remote(src, dst, send_sem, recv_sem, target):
    return pltpu.make_async_remote_copy(
        src_ref=src, dst_ref=dst, send_sem=send_sem, recv_sem=recv_sem, device_id=target, device_id_type=MESH
    )


def kernel(
    dims,
    patches_hbm, start_ref, length_ref, slot_ref, image_ref, gain_ref, wqkv_hbm, qgain_ref, kgain_ref, wout_hbm,
    packed_hbm, attended_hbm,
    blocks, normed, gathered, w_qkv, w_out, stats, mean_col, rstd_col, square, tables, dest_ref,
    pick_ref, run_send, run_recv, place_ref, packed_v,
    chosen, ordered, pair_send, pair_recv, part_own, rs_send, rs_recv, proj_own,
    q_ref, k_ref, v_ref, mask_ref, context, out_send, out_recv, out_own, attended_v,
    load_sem, wload_sem, store_sem, stat_s, stat_r, tab_s, tab_r, run_s, run_r,
    right_s, right_r, left_s, left_r, norm_s, norm_r, pair_s, pair_r, rs_s, rs_r, out_s, out_r,
):
    n_dp, Z, T, FL, KS, NH, HS, R, SUB, cap = dims
    C = n_dp // 2
    HL = NH // HS
    NCH = T // R
    SR = T // SUB
    D = FL * Z
    NT = min(512, NH)
    d, z = lax.axis_index("dp"), lax.axis_index("mp")
    c, j = d // 2, d % 2
    sibling = (d + 1 - 2 * j, z)

    load = pltpu.make_async_copy(patches_hbm, blocks.at[z], load_sem)
    load.start()
    barrier = pltpu.get_barrier_semaphore()
    for k in range(1, n_dp):
        pl.semaphore_signal(barrier, inc=1, device_id=(lax.rem(d + k, n_dp), z), device_id_type=MESH)
    for k in range(1, Z):
        pl.semaphore_signal(barrier, inc=1, device_id=(d, lax.rem(z + k, Z)), device_id_type=MESH)

    tables[d] = jnp.zeros((8, 128), I32)
    tables[d, 0:1, 0:n_dp] = start_ref[...]
    tables[d, 1:2, 0:n_dp] = length_ref[...]
    tables[d, 2:3, 0:n_dp] = slot_ref[...]
    load.wait()
    weight_load = pltpu.make_async_copy(wqkv_hbm, w_qkv, wload_sem.at[0])
    weight_load.start()
    out_loads = [
        pltpu.make_async_copy(wout_hbm.at[:, pl.ds(m * FL, FL)], w_out.at[m], wload_sem.at[1 + m]) for m in range(Z)
    ]
    for cp in out_loads:
        cp.start()
    x = blocks[z].astype(F32)
    stats[z] = jnp.zeros((8, 128), F32)
    stats[z, 0:1, :] = jnp.broadcast_to(jnp.sum(x, axis=-1, keepdims=True), (T, 128)).T[0:1, :]
    stats[z, 1:2, :] = jnp.broadcast_to(jnp.sum(x * x, axis=-1, keepdims=True), (T, 128)).T[0:1, :]
    pl.semaphore_wait(barrier, n_dp - 1 + Z - 1)

    def stat_copy(k):
        return remote(stats.at[z], stats.at[z], stat_s.at[k], stat_r.at[k], (d, lax.rem(z + k, Z)))

    def right_copy(s, i):
        block = blocks.at[z - s, pl.ds(i * SR, SR)]
        return remote(block, block, right_s.at[s, i], right_r.at[s + 1, i], (d, z + 1))

    def left_copy(s, i):
        block = blocks.at[z + s, pl.ds(i * SR, SR)]
        return remote(block, block, left_s.at[s, i], left_r.at[s + 1, i], (d, z - 1))

    def start_own(i):
        @pl.when(z + 1 < Z)
        def _():
            right_copy(0, i).start()

        @pl.when(z > 0)
        def _():
            left_copy(0, i).start()

    def tab_copy(k):
        return remote(tables.at[d], tables.at[d], tab_s.at[k], tab_r.at[k], (lax.rem(d + k, n_dp), z))

    def run_copy(k):
        t = lax.rem(d + k, n_dp)
        return remote(run_send.at[t], run_recv.at[d], run_s.at[k], run_r.at[k], (t, z))

    for k in range(1, Z):
        stat_copy(k).start()
    start_own(0)
    start_own(1)
    for k in range(1, n_dp):
        tab_copy(k).start()

    within = lax.broadcasted_iota(I32, (cap, T), 0)
    lane = lax.broadcasted_iota(I32, (cap, T), 1)
    for p in range(n_dp):
        hit = (within + start_ref[0:1, p : p + 1] == lane) & (within < length_ref[0:1, p : p + 1])
        pick_ref[p * cap : (p + 1) * cap, :] = hit.astype(F32).astype(BF16)
    run_send[...] = (
        jnp.dot(pick_ref[...], blocks[z], preferred_element_type=F32).astype(BF16).reshape(n_dp, cap, FL)
    )
    run_recv[d] = run_send[d]
    for k in range(1, n_dp):
        run_copy(k).start()

    for k in range(1, Z):
        stat_copy(k).wait()
    total = jnp.sum(stats[...], axis=0) * (1.0 / D)
    mean_row = total[0:1, :]
    rstd_row = lax.rsqrt(total[1:2, :] - mean_row * mean_row + epsilon)
    mean_col[...] = jnp.broadcast_to(mean_row, (T, 128)).T
    rstd_col[...] = jnp.broadcast_to(rstd_row, (T, 128)).T

    def norm_copy(m, h, i):
        rows = pl.ds(i * SR, SR)
        return remote(
            normed.at[m, h, rows], gathered.at[d, rows], norm_s.at[m, h, i], norm_r.at[d, i], (2 * m + h, z)
        )

    def spread(m, i):
        rows = pl.ds(i * SR, SR)
        gain = gain_ref[:, pl.ds(pl.multiple_of(m * FL, 128), FL)]
        raw = blocks[m, rows, :].astype(F32)
        done = ((raw - mean_col[rows, 0:1]) * rstd_col[rows, 0:1] * gain).astype(BF16)
        for h in range(2):
            normed[m, h, rows, :] = done[:, h * KS : (h + 1) * KS]

            @pl.when(2 * m + h != d)
            def _():
                norm_copy(m, h, i).start()

            @pl.when(2 * m + h == d)
            def _():
                gathered[d, rows, :] = normed[m, h, rows, :]

    for i in range(SUB):
        spread(z, i)

        @pl.loop(1, Z)
        def _(s):
            @pl.when(z - s >= 0)
            def _():
                right_copy(s - 1, i).wait_recv()

                @pl.when(z + 1 < Z)
                def _():
                    right_copy(s, i).start()

            @pl.when(z + s < Z)
            def _():
                left_copy(s - 1, i).wait_recv()

                @pl.when(z > 0)
                def _():
                    left_copy(s, i).start()

            @pl.when(z - s >= 0)
            def _():
                spread(z - s, i)

            @pl.when(z + s < Z)
            def _():
                spread(z + s, i)

        if i + 2 < SUB:
            start_own(i + 2)

    for k in range(1, n_dp):
        tab_copy(k).wait()
    starts, lengths = tables[:, 0, :], tables[:, 1, :]
    square[...] = jnp.zeros((128, 128), F32)
    square[0:n_dp, :] = tables[:, 2, :].astype(F32)
    slots = square[...].T[0:n_dp, :].astype(I32)
    u = lax.broadcasted_iota(I32, (n_dp, T), 1)
    dest = jnp.zeros((n_dp, T), I32)
    for p in range(n_dp):
        first = starts[:, p : p + 1]
        inside = (u >= first) & (u < first + lengths[:, p : p + 1])
        dest = dest + jnp.where(inside, u + (slots[:, p : p + 1] - first + p * T), 0)
    dest_ref[...] = dest

    same = jnp.broadcast_to(image_ref[...].astype(F32), (T, T))
    mask_ref[...] = (same == same.T).astype(F32)
    k_ref[...] = jnp.zeros_like(k_ref)
    v_ref[...] = jnp.zeros_like(v_ref)

    def wait_gathered(k, i):
        t = lax.rem(d + k, n_dp)
        rows = pl.ds(i * SR, SR)
        remote(normed.at[0, 0, rows], gathered.at[t, rows], norm_s.at[0, 0, i], norm_r.at[t, i], (t, z)).wait_recv()

    for i in range(SUB):

        @pl.loop(1, n_dp)
        def _(k):
            wait_gathered(k, i)

    CR = C * R
    weight_load.wait()

    def pair_copy(r):
        return remote(pair_send.at[r], pair_recv.at[r], pair_s.at[r], pair_r.at[r], sibling)

    def rs_copy(r, k):
        e = lax.rem(c + k, C)
        return remote(rs_send.at[r, k], rs_recv.at[r, k], rs_s.at[r, k], rs_r.at[r, k], (2 * e + j, z))

    def order(r, q):
        row = lax.broadcasted_iota(I32, (CR, T), 0)
        goal = (row // R) * (2 * T) + row % R + (q * T + r * R)
        for s in range(n_dp):
            chosen[:, s * T : (s + 1) * T] = (dest_ref[s : s + 1, :] == goal).astype(F32).astype(BF16)
        ordered[...] = jnp.dot(
            chosen[...], gathered[...].reshape(n_dp * T, KS), preferred_element_type=F32
        ).astype(BF16)

    def project(store):
        for part in range(3):

            @pl.loop(0, NH // NT)
            def _(n):
                cols = pl.ds(pl.multiple_of(n * NT, 128), NT)
                store(part, cols, jnp.dot(ordered[...], w_qkv[part, :, cols], preferred_element_type=F32))

    @pl.loop(0, NCH)
    def _(r):
        order(r, 1 - j)

        def store_pair(part, cols, y):
            pair_send[r, part, :, cols] = y.astype(BF16)

        project(store_pair)
        pair_copy(r).start()
        order(r, j)

        def store_own(part, cols, y):
            part_own[part, :, cols] = y

        project(store_own)
        pair_copy(r).wait_recv()
        for k in range(C):
            e = lax.rem(c + k, C)
            rows = pl.ds(pl.multiple_of(e * R, R), R)
            for part in range(3):
                y = part_own[part, rows, :] + pair_recv[r, part, rows, :].astype(F32)
                if k == 0:
                    proj_own[r, part] = y
                else:
                    rs_send[r, k, part] = y.astype(BF16)
            if k > 0:
                rs_copy(r, k).start()

    def out_copy(a, k):
        rows = pl.ds(pl.multiple_of(a * R, R), R)
        return remote(
            out_send.at[k, rows], out_recv.at[k, rows], out_s.at[k, a], out_r.at[k, a], (d, lax.rem(z + k, Z))
        )

    def receive(r):
        rows = pl.ds(pl.multiple_of(r * R, R), R)
        for k in range(1, C):
            rs_copy(r, k).wait_recv()
        for part in range(3):
            y = proj_own[r, part]
            for k in range(1, C):
                y = y + rs_recv[r, k, part].astype(F32)
            for h in range(HL):
                cols = slice(h * HS, (h + 1) * HS)
                if part == 0:
                    q_ref[rows, cols] = row_norm(y[:, cols], qgain_ref[...]).astype(BF16)
                elif part == 1:
                    k_ref[rows, cols] = row_norm(y[:, cols], kgain_ref[...]).astype(BF16)
                else:
                    v_ref[rows, cols] = y[:, cols].astype(BF16)

    def attend(a):
        rows = pl.ds(pl.multiple_of(a * R, R), R)
        same_image = mask_ref[rows, :] > 0.5
        for h in range(HL):
            cols = slice(h * HS, (h + 1) * HS)
            scores = lax.dot_general(
                q_ref[rows, cols], k_ref[:, cols], (((1,), (1,)), ((), ())), preferred_element_type=F32
            ) * HS ** (-0.5)
            raw = jnp.where(same_image, jnp.exp(scores), 0.0)
            attention = (raw / jnp.sum(raw, axis=-1, keepdims=True)).astype(BF16)
            context[:, cols] = jnp.dot(attention, v_ref[:, cols], preferred_element_type=F32).astype(BF16)
        for k in list(range(1, Z)) + [0]:
            m = lax.rem(z + k, Z)
            y = jnp.dot(context[...], w_out[m], preferred_element_type=F32).astype(BF16)
            if k == 0:
                out_own[rows, :] = y
            else:
                out_send[k, rows, :] = y
                out_copy(a, k).start()

    receive(0)
    for cp in out_loads:
        cp.wait()

    @pl.loop(1, NCH)
    def _(r):
        receive(r)
        attend(r - 1)

    attend(NCH - 1)

    for k in range(1, n_dp):
        run_copy(k).wait()
    spot = lax.broadcasted_iota(I32, (1, n_dp * cap), 1)
    goal = spot % cap
    for s in range(n_dp):
        goal = goal + jnp.where(spot // cap == s, slot_ref[0:1, s : s + 1], 0)
    place_ref[...] = (lax.broadcasted_iota(I32, (T, n_dp * cap), 0) == goal).astype(F32).astype(BF16)
    packed_v[...] = jnp.dot(
        place_ref[...], run_recv[...].reshape(n_dp * cap, FL), preferred_element_type=F32
    ).astype(BF16)
    packed_store = pltpu.make_async_copy(packed_v, packed_hbm, store_sem.at[0])
    packed_store.start()

    for i in range(SUB):
        for s in range(Z - 1):

            @pl.when((z - s >= 0) & (z + 1 < Z))
            def _():
                right_copy(s, i).wait_send()

            @pl.when((z + s < Z) & (z > 0))
            def _():
                left_copy(s, i).wait_send()

        for m in range(Z):
            for h in range(2):

                @pl.when(2 * m + h != d)
                def _():
                    norm_copy(m, h, i).wait_send()

    for r in range(NCH):
        pair_copy(r).wait_send()
        for k in range(1, C):
            rs_copy(r, k).wait_send()

    for a in range(NCH):
        rows = slice(a * R, (a + 1) * R)
        y = out_own[rows, :].astype(F32)
        for k in range(1, Z):
            out_copy(a, k).wait()
            y = y + out_recv[k, rows, :].astype(F32)
        attended_v[rows, :] = y.astype(BF16)
    attended_store = pltpu.make_async_copy(attended_v, attended_hbm, store_sem.at[1])
    attended_store.start()
    packed_store.wait()
    attended_store.wait()


def on_device(
    n_dp, Z, patches, send_start, run_length, slot_start, image_ids, norm_gain, qkv_weight, query_gain, key_gain, out_weight
):
    T, FL = patches.shape
    KS, _, NH = qkv_weight.shape
    HS = query_gain.shape[0]
    C = n_dp // 2
    R, SUB = 32, 4
    NCH = T // R
    cap = max(16, 2 * T // n_dp)
    dims = (n_dp, Z, T, FL, KS, NH, HS, R, SUB, cap)
    dma = pltpu.SemaphoreType.DMA
    vmem = pltpu.VMEM
    scratch = [
        vmem((Z, T, FL), BF16),
        vmem((Z, 2, T, KS), BF16),
        vmem((n_dp, T, KS), BF16),
        vmem((3, KS, NH), BF16),
        vmem((Z, NH, FL), BF16),
        vmem((Z, 8, 128), F32),
        vmem((T, 128), F32),
        vmem((T, 128), F32),
        vmem((128, 128), F32),
        vmem((n_dp, 8, 128), I32),
        vmem((n_dp, T), I32),
        vmem((n_dp * cap, T), BF16),
        vmem((n_dp, cap, FL), BF16),
        vmem((n_dp, cap, FL), BF16),
        vmem((T, n_dp * cap), BF16),
        vmem((T, FL), BF16),
        vmem((C * R, n_dp * T), BF16),
        vmem((C * R, KS), BF16),
        vmem((NCH, 3, C * R, NH), BF16),
        vmem((NCH, 3, C * R, NH), BF16),
        vmem((3, C * R, NH), F32),
        vmem((NCH, C, 3, R, NH), BF16),
        vmem((NCH, C, 3, R, NH), BF16),
        vmem((NCH, 3, R, NH), F32),
        vmem((T, NH), BF16),
        vmem((T, NH), BF16),
        vmem((T, NH), BF16),
        vmem((T, T), F32),
        vmem((R, NH), BF16),
        vmem((Z, T, FL), BF16),
        vmem((Z, T, FL), BF16),
        vmem((T, FL), BF16),
        vmem((T, FL), BF16),
        dma,
        dma((1 + Z,)),
        dma((2,)),
        dma((Z,)), dma((Z,)),
        dma((n_dp,)), dma((n_dp,)),
        dma((n_dp,)), dma((n_dp,)),
        dma((Z + 1, SUB)), dma((Z + 1, SUB)),
        dma((Z + 1, SUB)), dma((Z + 1, SUB)),
        dma((Z, 2, SUB)), dma((n_dp, SUB)),
        dma((NCH,)), dma((NCH,)),
        dma((NCH, C)), dma((NCH, C)),
        dma((Z, NCH)), dma((Z, NCH)),
    ]
    in_vmem = pl.BlockSpec(memory_space=pltpu.VMEM)
    anywhere = pl.BlockSpec(memory_space=pl.ANY)
    return pl.pallas_call(
        functools.partial(kernel, dims),
        out_shape=(jax.ShapeDtypeStruct((T, FL), BF16),) * 2,
        in_specs=[anywhere] + [in_vmem] * 5 + [anywhere] + [in_vmem] * 2 + [anywhere],
        out_specs=(anywhere,) * 2,
        scratch_shapes=scratch,
        compiler_params=pltpu.CompilerParams(
            collective_id=0, has_side_effects=True, vmem_limit_bytes=60 * 1024 * 1024
        ),
    )(
        patches, send_start, run_length, slot_start, image_ids, norm_gain.reshape(1, -1),
        jnp.transpose(qkv_weight, (1, 0, 2)), query_gain.reshape(1, -1), key_gain.reshape(1, -1), out_weight,
    )


def solution(mesh):
    n_dp, Z = mesh.shape["dp"], mesh.shape["mp"]
    assert n_dp == 2 * Z
    return jax.shard_map(
        functools.partial(on_device, n_dp, Z),
        mesh=mesh,
        in_specs=(
            P("dp", "mp"),
            P("dp", None),
            P("dp", None),
            P("dp", None),
            P("dp", None),
            P(),
            P("dp", None, "mp"),
            P(),
            P(),
            P("mp", None),
        ),
        out_specs=(P("dp", "mp"), P("dp", "mp")),
        check_vma=False,
    )
```

```python
import functools

import jax
import jax.numpy as jnp
from jax import lax
from jax.experimental import pallas as pl
from jax.experimental.pallas import tpu as pltpu
from jax.sharding import PartitionSpec as P

MESH = pl.DeviceIdType.MESH
F32, BF16, I32 = jnp.float32, jnp.bfloat16, jnp.int32
epsilon = 1e-06
to_pair, to_half, to_take = 2, 4, 7


def row_norm(values, scales):
    middle = jnp.mean(values, axis=-1, keepdims=True)
    spread = jnp.mean(values * values, axis=-1, keepdims=True) - middle * middle
    return (values - middle) * lax.rsqrt(spread + epsilon) * scales


def remote(src, dst, send_sem, recv_sem, target):
    return pltpu.make_async_remote_copy(
        src_ref=src, dst_ref=dst, send_sem=send_sem, recv_sem=recv_sem, device_id=target, device_id_type=MESH
    )


def kernel(
    dims,
    patches_hbm, start_ref, length_ref, slot_ref, image_ref, gain_ref, wqkv_hbm, qgain_ref, kgain_ref, wout_hbm,
    packed_hbm, attended_hbm,
    blocks, normed, gathered, w_qkv, w_out, stats, mean_col, rstd_col, square, tables, dest_ref,
    pick_ref, run_send, run_recv, place_ref, packed_v,
    chosen, ordered, pair_send, pair_recv, part_own, half_send, half_recv, held, rs_send, rs_recv, proj_own,
    q_ref, k_ref, v_ref, mask_ref, context, out_send, out_recv, end_recv, out_own, attended_v,
    load_sem, wload_sem, store_sem, stat_s, stat_r, tab_s, tab_r, run_s, run_r,
    block_s, block_r, relay_s, norm_s, norm_r, pair_s, pair_r, half_s, half_r, rs_s, rs_r, out_s, out_r, end_r,
):
    n_dp, Z, T, FL, KS, NH, HS, R, SUB, cap = dims
    C = n_dp // 2
    HL = NH // HS
    NCH = T // R
    SR = T // SUB
    D = FL * Z
    NT = min(512, NH)
    d, z = lax.axis_index("dp"), lax.axis_index("mp")
    c, j = d // 2, d % 2
    sibling = (d + 1 - 2 * j, z)

    load = pltpu.make_async_copy(patches_hbm, blocks.at[z], load_sem)
    load.start()
    barrier = pltpu.get_barrier_semaphore()
    for k in range(1, n_dp):
        pl.semaphore_signal(barrier, inc=1, device_id=(lax.rem(d + k, n_dp), z), device_id_type=MESH)
    for k in range(1, Z):
        pl.semaphore_signal(barrier, inc=1, device_id=(d, lax.rem(z + k, Z)), device_id_type=MESH)

    def stat_copy(k):
        return remote(stats.at[z], stats.at[z], stat_s.at[k], stat_r.at[k], (d, lax.rem(z + k, Z)))

    relayed = Z == 4

    def block_copy(m, i, target, send_sem):
        block = blocks.at[m, pl.ds(i * SR, SR)]
        return remote(block, block, send_sem, block_r.at[m, i], (d, target))

    def own_copy(k, i):
        rows = pl.ds(i * SR, SR)
        return remote(
            patches_hbm.at[rows], blocks.at[z, rows], block_s.at[k, i], block_r.at[z, i], (d, lax.rem(z + k, Z))
        )

    def own_goes(k):
        t = lax.rem(z + k, Z)
        return jnp.abs(t - z) < 3 if relayed else t >= 0

    def relay_copy(i):
        return block_copy(lax.rem(z + 2, Z), i, 3 * (z - 1), relay_s.at[i])

    middle = (z >= 1) & (z <= 2)

    def tab_copy(k):
        return remote(tables.at[d], tables.at[d], tab_s.at[k], tab_r.at[k], (lax.rem(d + k, n_dp), z))

    def run_copy(k):
        t = lax.rem(d + k, n_dp)
        return remote(run_send.at[t], run_recv.at[d], run_s.at[k], run_r.at[k], (t, z))

    pl.semaphore_wait(barrier, n_dp - 1 + Z - 1)
    def start_own(i):
        for k in sorted(range(1, Z), key=lambda k: abs(k - Z // 2)):

            @pl.when(own_goes(k))
            def _():
                own_copy(k, i).start()

    start_own(0)
    tables[d] = jnp.zeros((8, 128), I32)
    tables[d, 0:1, 0:n_dp] = start_ref[...]
    tables[d, 1:2, 0:n_dp] = length_ref[...]
    tables[d, 2:3, 0:n_dp] = slot_ref[...]
    load.wait()
    weight_load = pltpu.make_async_copy(wqkv_hbm, w_qkv, wload_sem.at[0])
    weight_load.start()
    out_loads = [
        pltpu.make_async_copy(wout_hbm.at[:, pl.ds(m * FL, FL)], w_out.at[m], wload_sem.at[1 + m]) for m in range(Z)
    ]
    for cp in out_loads:
        cp.start()
    x = blocks[z].astype(F32)
    stats[z] = jnp.zeros((8, 128), F32)
    stats[z, 0:1, :] = jnp.broadcast_to(jnp.sum(x, axis=-1, keepdims=True), (T, 128)).T[0:1, :]
    stats[z, 1:2, :] = jnp.broadcast_to(jnp.sum(x * x, axis=-1, keepdims=True), (T, 128)).T[0:1, :]
    for k in range(1, Z):
        stat_copy(k).start()
    for i in range(1, SUB):
        start_own(i)
    for k in range(1, n_dp):
        tab_copy(k).start()

    within = lax.broadcasted_iota(I32, (cap, T), 0)
    lane = lax.broadcasted_iota(I32, (cap, T), 1)
    for p in range(n_dp):
        hit = (within + start_ref[0:1, p : p + 1] == lane) & (within < length_ref[0:1, p : p + 1])
        pick_ref[p * cap : (p + 1) * cap, :] = hit.astype(F32).astype(BF16)
    run_send[...] = (
        jnp.dot(pick_ref[...], blocks[z], preferred_element_type=F32).astype(BF16).reshape(n_dp, cap, FL)
    )
    run_recv[d] = run_send[d]
    for k in range(1, n_dp):
        run_copy(k).start()

    for k in range(1, Z):
        stat_copy(k).wait()
    total = jnp.sum(stats[...], axis=0) * (1.0 / D)
    mean_row = total[0:1, :]
    rstd_row = lax.rsqrt(total[1:2, :] - mean_row * mean_row + epsilon)
    mean_col[...] = jnp.broadcast_to(mean_row, (T, 128)).T
    rstd_col[...] = jnp.broadcast_to(rstd_row, (T, 128)).T

    def norm_copy(m, h, i):
        rows = pl.ds(i * SR, SR)
        return remote(
            normed.at[m, h, rows], gathered.at[d, rows], norm_s.at[m, h, i], norm_r.at[d, i], (2 * m + h, z)
        )

    def spread(m, i):
        rows = pl.ds(i * SR, SR)
        gain = gain_ref[:, pl.ds(pl.multiple_of(m * FL, 128), FL)]
        raw = blocks[m, rows, :].astype(F32)
        done = ((raw - mean_col[rows, 0:1]) * rstd_col[rows, 0:1] * gain).astype(BF16)
        for h in range(2):
            normed[m, h, rows, :] = done[:, h * KS : (h + 1) * KS]

            @pl.when(2 * m + h != d)
            def _():
                norm_copy(m, h, i).start()

            @pl.when(2 * m + h == d)
            def _():
                gathered[d, rows, :] = normed[m, h, rows, :]

    def destinations():
        for k in range(1, n_dp):
            tab_copy(k).wait()
        starts, lengths = tables[:, 0, :], tables[:, 1, :]
        square[...] = jnp.zeros((128, 128), F32)
        square[0:n_dp, :] = tables[:, 2, :].astype(F32)
        slots = square[...].T[0:n_dp, :].astype(I32)
        u = lax.broadcasted_iota(I32, (n_dp, T), 1)
        dest = jnp.zeros((n_dp, T), I32)
        for p in range(n_dp):
            first = starts[:, p : p + 1]
            inside = (u >= first) & (u < first + lengths[:, p : p + 1])
            dest = dest + jnp.where(inside, u + (slots[:, p : p + 1] - first + p * T), 0)
        dest_ref[...] = dest

        same = jnp.broadcast_to(image_ref[...].astype(F32), (T, T))
        mask_ref[...] = (same == same.T).astype(F32)
        k_ref[...] = jnp.zeros_like(k_ref)
        v_ref[...] = jnp.zeros_like(v_ref)

    def place_runs():
        for k in range(1, n_dp):
            run_copy(k).wait()
        spot = lax.broadcasted_iota(I32, (1, n_dp * cap), 1)
        goal = spot % cap
        for s in range(n_dp):
            goal = goal + jnp.where(spot // cap == s, slot_ref[0:1, s : s + 1], 0)
        place_ref[...] = (lax.broadcasted_iota(I32, (T, n_dp * cap), 0) == goal).astype(F32).astype(BF16)
        packed_v[...] = jnp.dot(
            place_ref[...], run_recv[...].reshape(n_dp * cap, FL), preferred_element_type=F32
        ).astype(BF16)
        packed_store.start()

    packed_store = pltpu.make_async_copy(packed_v, packed_hbm, store_sem.at[0])

    def take(m, i):
        block_copy(m, i, z, relay_s.at[i]).wait_recv()

    for i in range(SUB):
        spread(z, i)
        if i == 1:
            destinations()
        if i == 2:
            place_runs()
        for s in [2, 1] + list(range(3, Z)):
            for m in (z - s, z + s):

                @pl.when((m >= 0) & (m < Z))
                def _():
                    take(m, i)

                    if relayed and s == 2:

                        @pl.when(middle)
                        def _():
                            relay_copy(i).start()

                    spread(m, i)

    def wait_gathered(k, i):
        t = lax.rem(d + k, n_dp)
        rows = pl.ds(i * SR, SR)
        remote(normed.at[0, 0, rows], gathered.at[t, rows], norm_s.at[0, 0, i], norm_r.at[t, i], (t, z)).wait_recv()

    for i in range(SUB):

        @pl.loop(1, n_dp)
        def _(k):
            wait_gathered(k, i)

    CR = C * R
    U = 3 * NCH
    H = NH // 2
    grid = C == 4
    across = c + 1 - 2 * (c % 2), c + 2 - 4 * (c // 2)
    weight_load.wait()

    def pair_copy(u):
        return remote(pair_send.at[u], pair_recv.at[u], pair_s.at[u], pair_r.at[u], sibling)

    def half_copy(u, n):
        return remote(half_send.at[u, n], half_recv.at[u, n], half_s.at[u, n], half_r.at[u, n], (2 * across[n] + j, z))

    def rs_copy(u, n):
        chip = across[n] if grid else lax.rem(c + n + 1, C)
        return remote(rs_send.at[u, n], rs_recv.at[u, n], rs_s.at[u, n], rs_r.at[u, n], (2 * chip + j, z))

    pieces = 2 if grid else C - 1

    def order(r):
        row = lax.broadcasted_iota(I32, (2 * CR, T), 0)
        side = row // CR
        row = row % CR
        goal = (row // R) * (2 * T) + row % R + r * R + T * (side * j + (1 - side) * (1 - j))
        for s in range(n_dp):
            chosen[:, s * T : (s + 1) * T] = (dest_ref[s : s + 1, :] == goal).astype(F32).astype(BF16)
        ordered[...] = jnp.dot(
            chosen[...], gathered[...].reshape(n_dp * T, KS), preferred_element_type=F32
        ).astype(BF16)

    def project(u):
        @pl.when(u % 3 == 0)
        def _():
            order(u // 3)

        @pl.loop(0, NH // NT)
        def _(n):
            cols = pl.ds(pl.multiple_of(n * NT, 128), NT)
            y = jnp.dot(ordered[...], w_qkv[(u + 1) % 3, :, cols], preferred_element_type=F32)
            pair_send[u, :, cols] = y[:CR].astype(BF16)
            part_own[u % (to_pair + 1), :, cols] = y[CR:]

        pair_copy(u).start()

    def add_pair(u):
        pair_copy(u).wait_recv()

        def total(chip):
            rows = pl.ds(pl.multiple_of(chip * R, R), R)
            return part_own[u % (to_pair + 1), rows, :] + pair_recv[u, rows, :].astype(F32)

        if grid:
            y = total(C - 1 - c)
            for n in range(2):
                half_send[u, n] = y[:, n * H : (n + 1) * H].astype(BF16)
                half_copy(u, n).start()
            for n in range(2):
                held[u % (to_half - to_pair + 1), n] = total(across[n])
        else:
            for n in range(pieces):
                rs_send[u, n] = total(lax.rem(c + n + 1, C)).astype(BF16)
                rs_copy(u, n).start()
        proj_own[u] = total(c)

    def add_half(u):
        if grid:
            for n in range(2):
                half_copy(u, 1 - n).wait_recv()
                near, other = slice((1 - n) * H, (2 - n) * H), slice(n * H, (n + 1) * H)
                rs_send[u, n, :, near] = (held[u % (to_half - to_pair + 1), n, :, near] + half_recv[u, 1 - n].astype(F32)).astype(BF16)
                rs_send[u, n, :, other] = held[u % (to_half - to_pair + 1), n, :, other].astype(BF16)
                rs_copy(u, n).start()

    def receive(u):
        rows = pl.ds(pl.multiple_of((u // 3) * R, R), R)
        for n in range(pieces):
            rs_copy(u, n).wait_recv()
        y = proj_own[u]
        for n in range(pieces):
            y = y + rs_recv[u, n].astype(F32)
        heads = [slice(h * HS, (h + 1) * HS) for h in range(HL)]

        @pl.when(u % 3 == 0)
        def _():
            for cols in heads:
                k_ref[rows, cols] = row_norm(y[:, cols], kgain_ref[...]).astype(BF16)

        @pl.when(u % 3 == 1)
        def _():
            v_ref[rows, :] = y.astype(BF16)

        @pl.when(u % 3 == 2)
        def _():
            for cols in heads:
                q_ref[rows, cols] = row_norm(y[:, cols], qgain_ref[...]).astype(BF16)

    inner = ((z + 1) // 2) % 2
    last = z // 3

    def out_copy(a, k):
        rows = pl.ds(pl.multiple_of(a * R, R), R)
        return remote(
            out_send.at[k, rows], out_recv.at[k, rows], out_s.at[k, a], out_r.at[k, a], (d, lax.rem(z + k, Z))
        )

    def end_copy(a, k):
        rows = pl.ds(pl.multiple_of(a * R, R), R)
        return remote(out_send.at[k, rows], end_recv.at[rows], out_s.at[k, a], end_r.at[a], (d, 1 + last))

    def attend(a):
        rows = pl.ds(pl.multiple_of(a * R, R), R)
        same_image = mask_ref[rows, :] > 0.5
        for h in range(HL):
            cols = slice(h * HS, (h + 1) * HS)
            scores = lax.dot_general(
                q_ref[rows, cols], k_ref[:, cols], (((1,), (1,)), ((), ())), preferred_element_type=F32
            ) * HS ** (-0.5)
            raw = jnp.where(same_image, jnp.exp(scores), 0.0)
            attention = (raw / jnp.sum(raw, axis=-1, keepdims=True)).astype(BF16)
            context[:, cols] = jnp.dot(attention, v_ref[:, cols], preferred_element_type=F32).astype(BF16)
        for t in range(Z):
            if t == Z - 1:
                k = 0
            elif relayed:
                k = inner * (1, 3, 2)[t] + (1 - inner) * ((1 - last) * (3 - t) + last * (1 + t))
            else:
                k = t + 1
            m = lax.rem(z + k, Z)
            y = jnp.dot(context[...], w_out[m], preferred_element_type=F32).astype(BF16)
            if t == Z - 1:
                out_own[rows, :] = y
            else:
                out_send[k, rows, :] = y
                if not relayed or t == 1:
                    out_copy(a, k).start()
                elif t == 0:

                    @pl.when(inner == 0)
                    def _():
                        end_copy(a, k).start()

                    @pl.when(inner == 1)
                    def _():
                        out_copy(a, k).start()

                else:

                    @pl.when(inner == 0)
                    def _():
                        out_copy(a, k).start()

    def pass_on(a):
        if relayed:

            @pl.when(inner == 1)
            def _():
                rows = pl.ds(pl.multiple_of(a * R, R), R)
                end_copy(a, 2).wait_recv()
                out_send[2, rows, :] = (
                    out_send[2, rows, :].astype(F32) + end_recv[rows, :].astype(F32)
                ).astype(BF16)
                out_copy(a, 2).start()

    for cp in out_loads:
        cp.wait()

    @pl.loop(0, U + to_take)
    def _(v):
        @pl.when(v < U)
        def _():
            project(v)

        @pl.when((v >= to_pair) & (v < U + to_pair))
        def _():
            add_pair(v - to_pair)

        @pl.when((v >= to_half) & (v < U + to_half))
        def _():
            add_half(v - to_half)

        @pl.when(v >= to_take)
        def _():
            u = v - to_take
            receive(u)

            @pl.when((u >= 7) & (u % 3 == 1))
            def _():
                pass_on((u - 7) // 3)

            @pl.when((u >= 4) & (u % 3 == 1))
            def _():
                attend((u - 4) // 3)

    pass_on(NCH - 2)
    attend(NCH - 1)
    pass_on(NCH - 1)

    for i in range(SUB):
        for k in range(1, Z):

            @pl.when(own_goes(k))
            def _():
                own_copy(k, i).wait_send()

        if relayed:

            @pl.when(middle)
            def _():
                relay_copy(i).wait_send()

        for m in range(Z):
            for h in range(2):

                @pl.when(2 * m + h != d)
                def _():
                    norm_copy(m, h, i).wait_send()

    @pl.loop(0, U)
    def _(u):
        pair_copy(u).wait_send()
        for n in range(pieces):
            rs_copy(u, n).wait_send()
        if grid:
            for n in range(2):
                half_copy(u, n).wait_send()

    for a in range(NCH):
        rows = slice(a * R, (a + 1) * R)
        y = out_own[rows, :].astype(F32)
        for k in range(1, Z):
            out_copy(a, k).wait_send()
            here = lax.rem(z + Z - k, Z) - z
            direct = (here < 3) & (here > -3) if relayed else here != 0

            @pl.when(direct)
            def _():
                out_copy(a, k).wait_recv()

            if relayed and k != 2:
                y = y + jnp.where(direct, out_recv[k, rows, :].astype(F32), 0.0)
            else:
                y = y + out_recv[k, rows, :].astype(F32)
        attended_v[rows, :] = y.astype(BF16)
    attended_store = pltpu.make_async_copy(attended_v, attended_hbm, store_sem.at[1])
    attended_store.start()
    packed_store.wait()
    attended_store.wait()


def on_device(
    n_dp, Z, patches, send_start, run_length, slot_start, image_ids, norm_gain, qkv_weight, query_gain, key_gain, out_weight
):
    T, FL = patches.shape
    KS, _, NH = qkv_weight.shape
    HS = query_gain.shape[0]
    C = n_dp // 2
    R, SUB = 32, 4
    NCH = T // R
    U, pieces = 3 * NCH, 2 if C == 4 else C - 1
    cap = max(16, 2 * T // n_dp)
    dims = (n_dp, Z, T, FL, KS, NH, HS, R, SUB, cap)
    dma = pltpu.SemaphoreType.DMA
    vmem = pltpu.VMEM
    scratch = [
        vmem((Z, T, FL), BF16),
        vmem((Z, 2, T, KS), BF16),
        vmem((n_dp, T, KS), BF16),
        vmem((3, KS, NH), BF16),
        vmem((Z, NH, FL), BF16),
        vmem((Z, 8, 128), F32),
        vmem((T, 128), F32),
        vmem((T, 128), F32),
        vmem((128, 128), F32),
        vmem((n_dp, 8, 128), I32),
        vmem((n_dp, T), I32),
        vmem((n_dp * cap, T), BF16),
        vmem((n_dp, cap, FL), BF16),
        vmem((n_dp, cap, FL), BF16),
        vmem((T, n_dp * cap), BF16),
        vmem((T, FL), BF16),
        vmem((2 * C * R, n_dp * T), BF16),
        vmem((2 * C * R, KS), BF16),
        vmem((U, C * R, NH), BF16),
        vmem((U, C * R, NH), BF16),
        vmem((to_pair + 1, C * R, NH), F32),
        vmem((U, 2, R, NH // 2), BF16),
        vmem((U, 2, R, NH // 2), BF16),
        vmem((to_half - to_pair + 1, 2, R, NH), F32),
        vmem((U, pieces, R, NH), BF16),
        vmem((U, pieces, R, NH), BF16),
        vmem((U, R, NH), F32),
        vmem((T, NH), BF16),
        vmem((T, NH), BF16),
        vmem((T, NH), BF16),
        vmem((T, T), F32),
        vmem((R, NH), BF16),
        vmem((Z, T, FL), BF16),
        vmem((Z, T, FL), BF16),
        vmem((T, FL), BF16),
        vmem((T, FL), BF16),
        vmem((T, FL), BF16),
        dma,
        dma((1 + Z,)),
        dma((2,)),
        dma((Z,)), dma((Z,)),
        dma((n_dp,)), dma((n_dp,)),
        dma((n_dp,)), dma((n_dp,)),
        dma((Z, SUB)), dma((Z, SUB)), dma((SUB,)),
        dma((Z, 2, SUB)), dma((n_dp, SUB)),
        dma((U,)), dma((U,)),
        dma((U, 2)), dma((U, 2)),
        dma((U, pieces)), dma((U, pieces)),
        dma((Z, NCH)), dma((Z, NCH)), dma((NCH,)),
    ]
    in_vmem = pl.BlockSpec(memory_space=pltpu.VMEM)
    anywhere = pl.BlockSpec(memory_space=pl.ANY)
    return pl.pallas_call(
        functools.partial(kernel, dims),
        out_shape=(jax.ShapeDtypeStruct((T, FL), BF16),) * 2,
        in_specs=[anywhere] + [in_vmem] * 5 + [anywhere] + [in_vmem] * 2 + [anywhere],
        out_specs=(anywhere,) * 2,
        scratch_shapes=scratch,
        compiler_params=pltpu.CompilerParams(
            collective_id=0, has_side_effects=True, vmem_limit_bytes=60 * 1024 * 1024
        ),
    )(
        patches, send_start, run_length, slot_start, image_ids, norm_gain.reshape(1, -1),
        jnp.transpose(qkv_weight, (1, 0, 2)), query_gain.reshape(1, -1), key_gain.reshape(1, -1), out_weight,
    )


def solution(mesh):
    n_dp, Z = mesh.shape["dp"], mesh.shape["mp"]
    assert n_dp == 2 * Z
    return jax.shard_map(
        functools.partial(on_device, n_dp, Z),
        mesh=mesh,
        in_specs=(
            P("dp", "mp"),
            P("dp", None),
            P("dp", None),
            P("dp", None),
            P("dp", None),
            P(),
            P("dp", None, "mp"),
            P(),
            P(),
            P("mp", None),
        ),
        out_specs=(P("dp", "mp"), P("dp", "mp")),
        check_vma=False,
    )
```

```python
import functools

import jax
import jax.numpy as jnp
from jax import lax
from jax.experimental import pallas as pl
from jax.experimental.pallas import tpu as pltpu
from jax.sharding import PartitionSpec as P

MESH = pl.DeviceIdType.MESH
F32, BF16, I32 = jnp.float32, jnp.bfloat16, jnp.int32
epsilon = 1e-06
to_pair, to_half, to_take = 2, 4, 7


def row_norm(values, scales):
    middle = jnp.mean(values, axis=-1, keepdims=True)
    spread = jnp.mean(values * values, axis=-1, keepdims=True) - middle * middle
    return (values - middle) * lax.rsqrt(spread + epsilon) * scales


def remote(src, dst, send_sem, recv_sem, target):
    return pltpu.make_async_remote_copy(
        src_ref=src, dst_ref=dst, send_sem=send_sem, recv_sem=recv_sem, device_id=target, device_id_type=MESH
    )


def kernel(
    dims,
    patches_hbm, start_ref, length_ref, slot_ref, image_ref, gain_ref, wqkv_hbm, qgain_ref, kgain_ref, wout_hbm,
    packed_hbm, attended_hbm,
    blocks, normed, gathered, w_qkv, w_out, stats, mean_col, rstd_col, square, tables, dest_ref,
    pick_ref, run_send, run_recv, place_ref, packed_v,
    chosen, ordered, pair_send, pair_recv, part_own, half_send, half_recv, held, rs_send, rs_recv, proj_own,
    q_ref, k_ref, v_ref, mask_ref, context, out_send, out_recv, end_recv, out_own, attended_v,
    load_sem, wload_sem, store_sem, stat_s, stat_r, tab_s, tab_r, run_s, run_r,
    block_s, block_r, relay_s, norm_s, norm_r, pair_s, pair_r, half_s, half_r, rs_s, rs_r, out_s, out_r, end_r,
):
    n_dp, Z, T, FL, KS, NH, HS, R, SUB, cap = dims
    C = n_dp // 2
    HL = NH // HS
    NCH = T // R
    SR = T // SUB
    D = FL * Z
    NT = min(512, NH)
    d, z = lax.axis_index("dp"), lax.axis_index("mp")
    c, j = d // 2, d % 2
    sibling = (d + 1 - 2 * j, z)

    load = pltpu.make_async_copy(patches_hbm, blocks.at[z], load_sem)
    load.start()
    barrier = pltpu.get_barrier_semaphore()
    for k in range(1, n_dp):
        pl.semaphore_signal(barrier, inc=1, device_id=(lax.rem(d + k, n_dp), z), device_id_type=MESH)
    for k in range(1, Z):
        pl.semaphore_signal(barrier, inc=1, device_id=(d, lax.rem(z + k, Z)), device_id_type=MESH)

    def stat_copy(k):
        return remote(stats.at[z], stats.at[z], stat_s.at[k], stat_r.at[k], (d, lax.rem(z + k, Z)))

    relayed = Z == 4

    def block_copy(m, i, target, send_sem):
        block = blocks.at[m, pl.ds(i * SR, SR)]
        return remote(block, block, send_sem, block_r.at[m, i], (d, target))

    def own_copy(k, i):
        rows = pl.ds(i * SR, SR)
        return remote(
            patches_hbm.at[rows], blocks.at[z, rows], block_s.at[k, i], block_r.at[z, i], (d, lax.rem(z + k, Z))
        )

    def own_goes(k):
        t = lax.rem(z + k, Z)
        return jnp.abs(t - z) < 3 if relayed else t >= 0

    def relay_copy(i):
        return block_copy(lax.rem(z + 2, Z), i, 3 * (z - 1), relay_s.at[i])

    middle = (z >= 1) & (z <= 2)

    def tab_copy(k):
        return remote(tables.at[d], tables.at[d], tab_s.at[k], tab_r.at[k], (lax.rem(d + k, n_dp), z))

    def run_copy(k):
        t = lax.rem(d + k, n_dp)
        return remote(run_send.at[t], run_recv.at[d], run_s.at[k], run_r.at[k], (t, z))

    pl.semaphore_wait(barrier, n_dp - 1 + Z - 1)
    def start_own(i):
        for k in sorted(range(1, Z), key=lambda k: abs(k - Z // 2)):

            @pl.when(own_goes(k))
            def _():
                own_copy(k, i).start()

    start_own(0)
    tables[d] = jnp.zeros((8, 128), I32)
    tables[d, 0:1, 0:n_dp] = start_ref[...]
    tables[d, 1:2, 0:n_dp] = length_ref[...]
    tables[d, 2:3, 0:n_dp] = slot_ref[...]
    load.wait()
    weight_load = pltpu.make_async_copy(wqkv_hbm, w_qkv, wload_sem.at[0])
    weight_load.start()
    out_loads = [
        pltpu.make_async_copy(wout_hbm.at[:, pl.ds(m * FL, FL)], w_out.at[m], wload_sem.at[1 + m]) for m in range(Z)
    ]
    for cp in out_loads:
        cp.start()
    x = blocks[z].astype(F32)
    stats[z] = jnp.zeros((8, 128), F32)
    stats[z, 0:1, :] = jnp.broadcast_to(jnp.sum(x, axis=-1, keepdims=True), (T, 128)).T[0:1, :]
    stats[z, 1:2, :] = jnp.broadcast_to(jnp.sum(x * x, axis=-1, keepdims=True), (T, 128)).T[0:1, :]
    for k in range(1, Z):
        stat_copy(k).start()
    for i in range(1, SUB):
        start_own(i)
    for k in range(1, n_dp):
        tab_copy(k).start()

    within = lax.broadcasted_iota(I32, (cap, T), 0)
    lane = lax.broadcasted_iota(I32, (cap, T), 1)
    for p in range(n_dp):
        hit = (within + start_ref[0:1, p : p + 1] == lane) & (within < length_ref[0:1, p : p + 1])
        pick_ref[p * cap : (p + 1) * cap, :] = hit.astype(F32).astype(BF16)
    run_send[...] = (
        jnp.dot(pick_ref[...], blocks[z], preferred_element_type=F32).astype(BF16).reshape(n_dp, cap, FL)
    )
    run_recv[d] = run_send[d]
    for k in range(1, n_dp):
        run_copy(k).start()

    for k in range(1, Z):
        stat_copy(k).wait()
    total = jnp.sum(stats[...], axis=0) * (1.0 / D)
    mean_row = total[0:1, :]
    rstd_row = lax.rsqrt(total[1:2, :] - mean_row * mean_row + epsilon)
    mean_col[...] = jnp.broadcast_to(mean_row, (T, 128)).T
    rstd_col[...] = jnp.broadcast_to(rstd_row, (T, 128)).T

    def norm_copy(m, h, i):
        rows = pl.ds(i * SR, SR)
        return remote(
            normed.at[m, h, rows], gathered.at[d, rows], norm_s.at[m, h, i], norm_r.at[d, i], (2 * m + h, z)
        )

    def spread(m, i):
        rows = pl.ds(i * SR, SR)
        gain = gain_ref[:, pl.ds(pl.multiple_of(m * FL, 128), FL)]
        raw = blocks[m, rows, :].astype(F32)
        done = ((raw - mean_col[rows, 0:1]) * rstd_col[rows, 0:1] * gain).astype(BF16)
        for h in range(2):
            normed[m, h, rows, :] = done[:, h * KS : (h + 1) * KS]

            @pl.when(2 * m + h != d)
            def _():
                norm_copy(m, h, i).start()

            @pl.when(2 * m + h == d)
            def _():
                gathered[d, rows, :] = normed[m, h, rows, :]

    def destinations():
        for k in range(1, n_dp):
            tab_copy(k).wait()
        starts, lengths = tables[:, 0, :], tables[:, 1, :]
        square[...] = jnp.zeros((128, 128), F32)
        square[0:n_dp, :] = tables[:, 2, :].astype(F32)
        slots = square[...].T[0:n_dp, :].astype(I32)
        u = lax.broadcasted_iota(I32, (n_dp, T), 1)
        dest = jnp.zeros((n_dp, T), I32)
        for p in range(n_dp):
            first = starts[:, p : p + 1]
            inside = (u >= first) & (u < first + lengths[:, p : p + 1])
            dest = dest + jnp.where(inside, u + (slots[:, p : p + 1] - first + p * T), 0)
        dest_ref[...] = dest

        same = jnp.broadcast_to(image_ref[...].astype(F32), (T, T))
        mask_ref[...] = (same == same.T).astype(F32)
        k_ref[...] = jnp.zeros_like(k_ref)
        v_ref[...] = jnp.zeros_like(v_ref)

    def place_runs():
        for k in range(1, n_dp):
            run_copy(k).wait()
        spot = lax.broadcasted_iota(I32, (1, n_dp * cap), 1)
        goal = spot % cap
        for s in range(n_dp):
            goal = goal + jnp.where(spot // cap == s, slot_ref[0:1, s : s + 1], 0)
        place_ref[...] = (lax.broadcasted_iota(I32, (T, n_dp * cap), 0) == goal).astype(F32).astype(BF16)
        packed_v[...] = jnp.dot(
            place_ref[...], run_recv[...].reshape(n_dp * cap, FL), preferred_element_type=F32
        ).astype(BF16)
        packed_store.start()

    packed_store = pltpu.make_async_copy(packed_v, packed_hbm, store_sem.at[0])

    def take(m, i):
        block_copy(m, i, z, relay_s.at[i]).wait_recv()

    for i in range(SUB):
        spread(z, i)
        if i == 1:
            destinations()
        if i == 2:
            place_runs()
        for s in [2, 1] + list(range(3, Z)):
            for m in (z - s, z + s):

                @pl.when((m >= 0) & (m < Z))
                def _():
                    take(m, i)

                    if relayed and s == 2:

                        @pl.when(middle)
                        def _():
                            relay_copy(i).start()

                    spread(m, i)

    def wait_gathered(k, i):
        t = lax.rem(d + k, n_dp)
        rows = pl.ds(i * SR, SR)
        remote(normed.at[0, 0, rows], gathered.at[t, rows], norm_s.at[0, 0, i], norm_r.at[t, i], (t, z)).wait_recv()

    for i in range(SUB):

        @pl.loop(1, n_dp)
        def _(k):
            wait_gathered(k, i)

    CR = C * R
    U = 3 * NCH
    H = NH // 2
    grid = C == 4
    across = c + 1 - 2 * (c % 2), c + 2 - 4 * (c // 2)
    weight_load.wait()

    def pair_copy(u):
        return remote(pair_send.at[u], pair_recv.at[u], pair_s.at[u], pair_r.at[u], sibling)

    def half_copy(u, n):
        return remote(half_send.at[u, n], half_recv.at[u, n], half_s.at[u, n], half_r.at[u, n], (2 * across[n] + j, z))

    def rs_copy(u, n):
        chip = across[n] if grid else lax.rem(c + n + 1, C)
        return remote(rs_send.at[u, n], rs_recv.at[u, n], rs_s.at[u, n], rs_r.at[u, n], (2 * chip + j, z))

    pieces = 2 if grid else C - 1

    def order(r):
        row = lax.broadcasted_iota(I32, (2 * CR, T), 0)
        side = row // CR
        row = row % CR
        goal = (row // R) * (2 * T) + row % R + r * R + T * (side * j + (1 - side) * (1 - j))
        for s in range(n_dp):
            chosen[:, s * T : (s + 1) * T] = (dest_ref[s : s + 1, :] == goal).astype(F32).astype(BF16)
        ordered[...] = jnp.dot(
            chosen[...], gathered[...].reshape(n_dp * T, KS), preferred_element_type=F32
        ).astype(BF16)

    def project(u):
        @pl.when(u % 3 == 0)
        def _():
            order(u // 3)

        @pl.loop(0, NH // NT)
        def _(n):
            cols = pl.ds(pl.multiple_of(n * NT, 128), NT)
            y = jnp.dot(ordered[...], w_qkv[(u + 1) % 3, :, cols], preferred_element_type=F32)
            pair_send[u, :, cols] = y[:CR].astype(BF16)
            part_own[u % (to_pair + 1), :, cols] = y[CR:]

        pair_copy(u).start()

    def add_pair(u):
        pair_copy(u).wait_recv()

        def total(chip):
            rows = pl.ds(pl.multiple_of(chip * R, R), R)
            return part_own[u % (to_pair + 1), rows, :] + pair_recv[u, rows, :].astype(F32)

        if grid:
            y = total(C - 1 - c)
            for n in range(2):
                half_send[u, n] = y[:, n * H : (n + 1) * H].astype(BF16)
                half_copy(u, n).start()
            for n in range(2):
                held[u % (to_half - to_pair + 1), n] = total(across[n])
        else:
            for n in range(pieces):
                rs_send[u, n] = total(lax.rem(c + n + 1, C)).astype(BF16)
                rs_copy(u, n).start()
        proj_own[u] = total(c)

    def add_half(u):
        if grid:
            for n in range(2):
                half_copy(u, 1 - n).wait_recv()
                near, other = slice((1 - n) * H, (2 - n) * H), slice(n * H, (n + 1) * H)
                rs_send[u, n, :, near] = (held[u % (to_half - to_pair + 1), n, :, near] + half_recv[u, 1 - n].astype(F32)).astype(BF16)
                rs_send[u, n, :, other] = held[u % (to_half - to_pair + 1), n, :, other].astype(BF16)
                rs_copy(u, n).start()

    def receive(u):
        rows = pl.ds(pl.multiple_of((u // 3) * R, R), R)
        for n in range(pieces):
            rs_copy(u, n).wait_recv()
        y = proj_own[u]
        for n in range(pieces):
            y = y + rs_recv[u, n].astype(F32)
        heads = [slice(h * HS, (h + 1) * HS) for h in range(HL)]

        @pl.when(u % 3 == 0)
        def _():
            for cols in heads:
                k_ref[rows, cols] = row_norm(y[:, cols], kgain_ref[...]).astype(BF16)

        @pl.when(u % 3 == 1)
        def _():
            v_ref[rows, :] = y.astype(BF16)

        @pl.when(u % 3 == 2)
        def _():
            for cols in heads:
                q_ref[rows, cols] = row_norm(y[:, cols], qgain_ref[...]).astype(BF16)

    inner = ((z + 1) // 2) % 2
    last = z // 3

    def out_copy(a, k):
        rows = pl.ds(pl.multiple_of(a * R, R), R)
        return remote(
            out_send.at[k, rows], out_recv.at[k, rows], out_s.at[k, a], out_r.at[k, a], (d, lax.rem(z + k, Z))
        )

    def end_copy(a, k):
        rows = pl.ds(pl.multiple_of(a * R, R), R)
        return remote(out_send.at[k, rows], end_recv.at[rows], out_s.at[k, a], end_r.at[a], (d, 1 + last))

    def attend(a):
        rows = pl.ds(pl.multiple_of(a * R, R), R)
        same_image = mask_ref[rows, :] > 0.5
        heads = [slice(h * HS, (h + 1) * HS) for h in range(HL)]
        scores = [
            lax.dot_general(
                q_ref[rows, cols], k_ref[:, cols], (((1,), (1,)), ((), ())), preferred_element_type=F32
            )
            for cols in heads
        ]
        raw = [jnp.where(same_image, jnp.exp(s * HS ** (-0.5)), 0.0) for s in scores]
        totals = [jnp.sum(w, axis=-1, keepdims=True) for w in raw]
        attention = [(w / total).astype(BF16) for w, total in zip(raw, totals)]
        terms = [
            jnp.dot(w, v_ref[:, cols], preferred_element_type=F32).astype(BF16) for w, cols in zip(attention, heads)
        ]
        for term, cols in zip(terms, heads):
            context[:, cols] = term
        for t in range(Z):
            if t == Z - 1:
                k = 0
            elif relayed:
                k = inner * (1, 3, 2)[t] + (1 - inner) * ((1 - last) * (3 - t) + last * (1 + t))
            else:
                k = t + 1
            m = lax.rem(z + k, Z)
            y = jnp.dot(context[...], w_out[m], preferred_element_type=F32).astype(BF16)
            if t == Z - 1:
                out_own[rows, :] = y
            else:
                out_send[k, rows, :] = y
                if not relayed or t == 1:
                    out_copy(a, k).start()
                elif t == 0:

                    @pl.when(inner == 0)
                    def _():
                        end_copy(a, k).start()

                    @pl.when(inner == 1)
                    def _():
                        out_copy(a, k).start()

                else:

                    @pl.when(inner == 0)
                    def _():
                        out_copy(a, k).start()

    def pass_on(a):
        if relayed:

            @pl.when(inner == 1)
            def _():
                rows = pl.ds(pl.multiple_of(a * R, R), R)
                end_copy(a, 2).wait_recv()
                out_send[2, rows, :] = (
                    out_send[2, rows, :].astype(F32) + end_recv[rows, :].astype(F32)
                ).astype(BF16)
                out_copy(a, 2).start()

    for cp in out_loads:
        cp.wait()

    @pl.loop(0, U + to_take)
    def _(v):
        @pl.when(v < U)
        def _():
            project(v)

        @pl.when((v >= to_pair) & (v < U + to_pair))
        def _():
            add_pair(v - to_pair)

        @pl.when((v >= to_half) & (v < U + to_half))
        def _():
            add_half(v - to_half)

        @pl.when(v >= to_take)
        def _():
            u = v - to_take
            receive(u)

            @pl.when((u >= 7) & (u % 3 == 1))
            def _():
                pass_on((u - 7) // 3)

            @pl.when((u >= 4) & (u % 3 == 1))
            def _():
                attend((u - 4) // 3)

    pass_on(NCH - 2)
    attend(NCH - 1)
    pass_on(NCH - 1)

    for i in range(SUB):
        for k in range(1, Z):

            @pl.when(own_goes(k))
            def _():
                own_copy(k, i).wait_send()

        if relayed:

            @pl.when(middle)
            def _():
                relay_copy(i).wait_send()

        for m in range(Z):
            for h in range(2):

                @pl.when(2 * m + h != d)
                def _():
                    norm_copy(m, h, i).wait_send()

    @pl.loop(0, U)
    def _(u):
        pair_copy(u).wait_send()
        for n in range(pieces):
            rs_copy(u, n).wait_send()
        if grid:
            for n in range(2):
                half_copy(u, n).wait_send()

    for a in range(NCH):
        rows = slice(a * R, (a + 1) * R)
        y = out_own[rows, :].astype(F32)
        for k in range(1, Z):
            out_copy(a, k).wait_send()
            here = lax.rem(z + Z - k, Z) - z
            direct = (here < 3) & (here > -3) if relayed else here != 0

            @pl.when(direct)
            def _():
                out_copy(a, k).wait_recv()

            if relayed and k != 2:
                y = y + jnp.where(direct, out_recv[k, rows, :].astype(F32), 0.0)
            else:
                y = y + out_recv[k, rows, :].astype(F32)
        attended_v[rows, :] = y.astype(BF16)
    attended_store = pltpu.make_async_copy(attended_v, attended_hbm, store_sem.at[1])
    attended_store.start()
    packed_store.wait()
    attended_store.wait()


def hand_over(packed_in, attended_in, packed_out, attended_out):
    packed_out[...] = packed_in[...]
    attended_out[...] = attended_in[...]


def on_device(
    n_dp, Z, patches, send_start, run_length, slot_start, image_ids, norm_gain, qkv_weight, query_gain, key_gain, out_weight
):
    T, FL = patches.shape
    KS, _, NH = qkv_weight.shape
    HS = query_gain.shape[0]
    C = n_dp // 2
    R, SUB = 32, 4
    NCH = T // R
    U, pieces = 3 * NCH, 2 if C == 4 else C - 1
    cap = max(16, 2 * T // n_dp)
    dims = (n_dp, Z, T, FL, KS, NH, HS, R, SUB, cap)
    dma = pltpu.SemaphoreType.DMA
    vmem = pltpu.VMEM
    scratch = [
        vmem((Z, T, FL), BF16),
        vmem((Z, 2, T, KS), BF16),
        vmem((n_dp, T, KS), BF16),
        vmem((3, KS, NH), BF16),
        vmem((Z, NH, FL), BF16),
        vmem((Z, 8, 128), F32),
        vmem((T, 128), F32),
        vmem((T, 128), F32),
        vmem((128, 128), F32),
        vmem((n_dp, 8, 128), I32),
        vmem((n_dp, T), I32),
        vmem((n_dp * cap, T), BF16),
        vmem((n_dp, cap, FL), BF16),
        vmem((n_dp, cap, FL), BF16),
        vmem((T, n_dp * cap), BF16),
        vmem((T, FL), BF16),
        vmem((2 * C * R, n_dp * T), BF16),
        vmem((2 * C * R, KS), BF16),
        vmem((U, C * R, NH), BF16),
        vmem((U, C * R, NH), BF16),
        vmem((to_pair + 1, C * R, NH), F32),
        vmem((U, 2, R, NH // 2), BF16),
        vmem((U, 2, R, NH // 2), BF16),
        vmem((to_half - to_pair + 1, 2, R, NH), F32),
        vmem((U, pieces, R, NH), BF16),
        vmem((U, pieces, R, NH), BF16),
        vmem((U, R, NH), F32),
        vmem((T, NH), BF16),
        vmem((T, NH), BF16),
        vmem((T, NH), BF16),
        vmem((T, T), F32),
        vmem((R, NH), BF16),
        vmem((Z, T, FL), BF16),
        vmem((Z, T, FL), BF16),
        vmem((T, FL), BF16),
        vmem((T, FL), BF16),
        vmem((T, FL), BF16),
        dma,
        dma((1 + Z,)),
        dma((2,)),
        dma((Z,)), dma((Z,)),
        dma((n_dp,)), dma((n_dp,)),
        dma((n_dp,)), dma((n_dp,)),
        dma((Z, SUB)), dma((Z, SUB)), dma((SUB,)),
        dma((Z, 2, SUB)), dma((n_dp, SUB)),
        dma((U,)), dma((U,)),
        dma((U, 2)), dma((U, 2)),
        dma((U, pieces)), dma((U, pieces)),
        dma((Z, NCH)), dma((Z, NCH)), dma((NCH,)),
    ]
    in_vmem = pl.BlockSpec(memory_space=pltpu.VMEM)
    anywhere = pl.BlockSpec(memory_space=pl.ANY)
    outs = pl.pallas_call(
        functools.partial(kernel, dims),
        out_shape=(jax.ShapeDtypeStruct((T, FL), BF16),) * 2,
        in_specs=[anywhere] + [in_vmem] * 5 + [anywhere] + [in_vmem] * 2 + [anywhere],
        out_specs=(anywhere,) * 2,
        scratch_shapes=scratch,
        compiler_params=pltpu.CompilerParams(
            collective_id=0, has_side_effects=True, vmem_limit_bytes=60 * 1024 * 1024
        ),
    )(
        patches, send_start, run_length, slot_start, image_ids, norm_gain.reshape(1, -1),
        jnp.transpose(qkv_weight, (1, 0, 2)), query_gain.reshape(1, -1), key_gain.reshape(1, -1), out_weight,
    )
    return tuple(
        pl.pallas_call(
            hand_over, out_shape=(jax.ShapeDtypeStruct((T, FL), BF16),) * 2, in_specs=[in_vmem] * 2, out_specs=(in_vmem,) * 2
        )(*outs)
    )


def solution(mesh):
    n_dp, Z = mesh.shape["dp"], mesh.shape["mp"]
    assert n_dp == 2 * Z
    return jax.shard_map(
        functools.partial(on_device, n_dp, Z),
        mesh=mesh,
        in_specs=(
            P("dp", "mp"),
            P("dp", None),
            P("dp", None),
            P("dp", None),
            P("dp", None),
            P(),
            P("dp", None, "mp"),
            P(),
            P(),
            P("mp", None),
        ),
        out_specs=(P("dp", "mp"), P("dp", "mp")),
        check_vma=False,
    )
```

```python
import functools

import jax
import jax.numpy as jnp
from jax import lax
from jax.experimental import pallas as pl
from jax.experimental.pallas import tpu as pltpu
from jax.sharding import PartitionSpec as P

MESH = pl.DeviceIdType.MESH
F32, BF16, I32 = jnp.float32, jnp.bfloat16, jnp.int32
epsilon = 1e-06
to_pair, to_half, to_take = 2, 4, 7


def row_norm(values, scales):
    middle = jnp.mean(values, axis=-1, keepdims=True)
    spread = jnp.mean(values * values, axis=-1, keepdims=True) - middle * middle
    return (values - middle) * lax.rsqrt(spread + epsilon) * scales


def remote(src, dst, send_sem, recv_sem, target):
    return pltpu.make_async_remote_copy(
        src_ref=src, dst_ref=dst, send_sem=send_sem, recv_sem=recv_sem, device_id=target, device_id_type=MESH
    )


def kernel(
    dims,
    patches_hbm, start_ref, length_ref, slot_ref, image_ref, gain_ref, wqkv_hbm, qgain_ref, kgain_ref, wout_hbm,
    packed_hbm, attended_hbm,
    blocks, normed, gathered, w_qkv, w_out, stats, mean_col, rstd_col, square, tables, dest_ref,
    pick_ref, run_send, run_recv, place_ref, packed_v,
    chosen, ordered, pair_send, pair_recv, part_own, half_send, half_recv, held, rs_send, rs_recv, proj_own,
    q_ref, k_ref, v_ref, mask_ref, context, out_send, out_recv, end_recv, out_own, attended_v,
    load_sem, wload_sem, store_sem, stat_s, stat_r, tab_s, tab_r, run_s, run_r,
    block_s, block_r, relay_s, norm_s, norm_r, pair_s, pair_r, half_s, half_r, rs_s, rs_r, out_s, out_r, end_r,
):
    n_dp, Z, T, FL, KS, NH, HS, R, SUB, cap = dims
    C = n_dp // 2
    HL = NH // HS
    NCH = T // R
    SR = T // SUB
    D = FL * Z
    NT = min(1024, NH)
    d, z = lax.axis_index("dp"), lax.axis_index("mp")
    c, j = d // 2, d % 2
    sibling = (d + 1 - 2 * j, z)

    load = pltpu.make_async_copy(patches_hbm, blocks.at[z], load_sem)
    load.start()
    barrier = pltpu.get_barrier_semaphore()
    for k in range(1, n_dp):
        pl.semaphore_signal(barrier, inc=1, device_id=(lax.rem(d + k, n_dp), z), device_id_type=MESH)
    for k in range(1, Z):
        pl.semaphore_signal(barrier, inc=1, device_id=(d, lax.rem(z + k, Z)), device_id_type=MESH)

    def stat_copy(k):
        return remote(stats.at[z], stats.at[z], stat_s.at[k], stat_r.at[k], (d, lax.rem(z + k, Z)))

    relayed = Z == 4

    def block_copy(m, i, target, send_sem):
        block = blocks.at[m, pl.ds(i * SR, SR)]
        return remote(block, block, send_sem, block_r.at[m, i], (d, target))

    def own_copy(k, i):
        rows = pl.ds(i * SR, SR)
        return remote(
            patches_hbm.at[rows], blocks.at[z, rows], block_s.at[k, i], block_r.at[z, i], (d, lax.rem(z + k, Z))
        )

    def own_goes(k):
        t = lax.rem(z + k, Z)
        return jnp.abs(t - z) < 3 if relayed else t >= 0

    def relay_copy(i):
        return block_copy(lax.rem(z + 2, Z), i, 3 * (z - 1), relay_s.at[i])

    middle = (z >= 1) & (z <= 2)

    def tab_copy(k):
        return remote(tables.at[d], tables.at[d], tab_s.at[k], tab_r.at[k], (lax.rem(d + k, n_dp), z))

    def run_copy(k):
        t = lax.rem(d + k, n_dp)
        return remote(run_send.at[t], run_recv.at[d], run_s.at[k], run_r.at[k], (t, z))

    pl.semaphore_wait(barrier, n_dp - 1 + Z - 1)
    def start_own(i):
        for k in sorted(range(1, Z), key=lambda k: abs(k - Z // 2)):

            @pl.when(own_goes(k))
            def _():
                own_copy(k, i).start()

    start_own(0)
    tables[d] = jnp.zeros((8, 128), I32)
    tables[d, 0:1, 0:n_dp] = start_ref[...]
    tables[d, 1:2, 0:n_dp] = length_ref[...]
    tables[d, 2:3, 0:n_dp] = slot_ref[...]
    load.wait()
    weight_load = pltpu.make_async_copy(wqkv_hbm, w_qkv, wload_sem.at[0])
    weight_load.start()
    out_loads = [
        pltpu.make_async_copy(wout_hbm.at[:, pl.ds(m * FL, FL)], w_out.at[m], wload_sem.at[1 + m]) for m in range(Z)
    ]
    for cp in out_loads:
        cp.start()
    x = blocks[z].astype(F32)
    stats[z] = jnp.zeros((8, 128), F32)
    stats[z, 0:1, :] = jnp.broadcast_to(jnp.sum(x, axis=-1, keepdims=True), (T, 128)).T[0:1, :]
    stats[z, 1:2, :] = jnp.broadcast_to(jnp.sum(x * x, axis=-1, keepdims=True), (T, 128)).T[0:1, :]
    for k in range(1, Z):
        stat_copy(k).start()
    for i in range(1, SUB):
        start_own(i)
    for k in range(1, n_dp):
        tab_copy(k).start()

    within = lax.broadcasted_iota(I32, (cap, T), 0)
    lane = lax.broadcasted_iota(I32, (cap, T), 1)
    for p in range(n_dp):
        hit = (within + start_ref[0:1, p : p + 1] == lane) & (within < length_ref[0:1, p : p + 1])
        pick_ref[p * cap : (p + 1) * cap, :] = hit.astype(F32).astype(BF16)
    run_send[...] = (
        jnp.dot(pick_ref[...], blocks[z], preferred_element_type=F32).astype(BF16).reshape(n_dp, cap, FL)
    )
    run_recv[d] = run_send[d]
    for k in range(1, n_dp):
        run_copy(k).start()

    for k in range(1, Z):
        stat_copy(k).wait()
    total = jnp.sum(stats[...], axis=0) * (1.0 / D)
    mean_row = total[0:1, :]
    rstd_row = lax.rsqrt(total[1:2, :] - mean_row * mean_row + epsilon)
    mean_col[...] = jnp.broadcast_to(mean_row, (T, 128)).T
    rstd_col[...] = jnp.broadcast_to(rstd_row, (T, 128)).T

    def norm_copy(m, h, i):
        rows = pl.ds(i * SR, SR)
        return remote(
            normed.at[m, h, rows], gathered.at[d, rows], norm_s.at[m, h, i], norm_r.at[d, i], (2 * m + h, z)
        )

    def spread(m, i):
        rows = pl.ds(i * SR, SR)
        gain = gain_ref[:, pl.ds(pl.multiple_of(m * FL, 128), FL)]
        raw = blocks[m, rows, :].astype(F32)
        done = ((raw - mean_col[rows, 0:1]) * rstd_col[rows, 0:1] * gain).astype(BF16)
        for h in range(2):
            normed[m, h, rows, :] = done[:, h * KS : (h + 1) * KS]

            @pl.when(2 * m + h != d)
            def _():
                norm_copy(m, h, i).start()

            @pl.when(2 * m + h == d)
            def _():
                gathered[d, rows, :] = normed[m, h, rows, :]

    def destinations():
        for k in range(1, n_dp):
            tab_copy(k).wait()
        starts, lengths = tables[:, 0, :], tables[:, 1, :]
        square[...] = jnp.zeros((128, 128), F32)
        square[0:n_dp, :] = tables[:, 2, :].astype(F32)
        slots = square[...].T[0:n_dp, :].astype(I32)
        u = lax.broadcasted_iota(I32, (n_dp, T), 1)
        dest = jnp.zeros((n_dp, T), I32)
        for p in range(n_dp):
            first = starts[:, p : p + 1]
            inside = (u >= first) & (u < first + lengths[:, p : p + 1])
            dest = dest + jnp.where(inside, u + (slots[:, p : p + 1] - first + p * T), 0)
        dest_ref[...] = dest

        same = jnp.broadcast_to(image_ref[...].astype(F32), (T, T))
        mask_ref[...] = (same == same.T).astype(F32)
        k_ref[...] = jnp.zeros_like(k_ref)
        v_ref[...] = jnp.zeros_like(v_ref)

    def place_runs():
        for k in range(1, n_dp):
            run_copy(k).wait()
        spot = lax.broadcasted_iota(I32, (1, n_dp * cap), 1)
        goal = spot % cap
        for s in range(n_dp):
            goal = goal + jnp.where(spot // cap == s, slot_ref[0:1, s : s + 1], 0)
        place_ref[...] = (lax.broadcasted_iota(I32, (T, n_dp * cap), 0) == goal).astype(F32).astype(BF16)
        packed_v[...] = jnp.dot(
            place_ref[...], run_recv[...].reshape(n_dp * cap, FL), preferred_element_type=F32
        ).astype(BF16)
        packed_store.start()

    packed_store = pltpu.make_async_copy(packed_v, packed_hbm, store_sem.at[0])

    def take(m, i):
        block_copy(m, i, z, relay_s.at[i]).wait_recv()

    for i in range(SUB):
        spread(z, i)
        if i == 1:
            destinations()
        if i == 2:
            place_runs()
        for s in [2, 1] + list(range(3, Z)):
            for m in (z - s, z + s):

                @pl.when((m >= 0) & (m < Z))
                def _():
                    take(m, i)

                    if relayed and s == 2:

                        @pl.when(middle)
                        def _():
                            relay_copy(i).start()

                    spread(m, i)

    CR = C * R

    def choose(r):
        row = lax.broadcasted_iota(I32, (2 * CR, T), 0)
        side = row // CR
        row = row % CR
        goal = (row // R) * (2 * T) + row % R + r * R + T * (side * j + (1 - side) * (1 - j))
        for s in range(n_dp):
            chosen[:, s * T : (s + 1) * T] = (dest_ref[s : s + 1, :] == goal).astype(F32).astype(BF16)

    choose(0)

    def wait_gathered(k, i):
        t = lax.rem(d + k, n_dp)
        rows = pl.ds(i * SR, SR)
        remote(normed.at[0, 0, rows], gathered.at[t, rows], norm_s.at[0, 0, i], norm_r.at[t, i], (t, z)).wait_recv()

    for i in range(SUB):

        @pl.loop(1, n_dp)
        def _(k):
            wait_gathered(k, i)

    U = 3 * NCH
    H = NH // 2
    grid = C == 4
    across = c + 1 - 2 * (c % 2), c + 2 - 4 * (c // 2)
    weight_load.wait()

    def pair_copy(u):
        return remote(pair_send.at[u], pair_recv.at[u], pair_s.at[u], pair_r.at[u], sibling)

    def half_copy(u, n):
        return remote(half_send.at[u, n], half_recv.at[u, n], half_s.at[u, n], half_r.at[u, n], (2 * across[n] + j, z))

    def rs_copy(u, n):
        chip = across[n] if grid else lax.rem(c + n + 1, C)
        return remote(rs_send.at[u, n], rs_recv.at[u, n], rs_s.at[u, n], rs_r.at[u, n], (2 * chip + j, z))

    pieces = 2 if grid else C - 1

    def project(u):
        @pl.when(u % 3 == 0)
        def _():
            ordered[...] = jnp.dot(
                chosen[...], gathered[...].reshape(n_dp * T, KS), preferred_element_type=F32
            ).astype(BF16)

        @pl.loop(0, NH // NT)
        def _(n):
            cols = pl.ds(pl.multiple_of(n * NT, 128), NT)
            y = jnp.dot(ordered[...], w_qkv[(u + 1) % 3, :, cols], preferred_element_type=F32)
            pair_send[u, :, cols] = y[:CR].astype(BF16)
            part_own[u % (to_pair + 1), :, cols] = y[CR:]

        pair_copy(u).start()

        @pl.when((u % 3 == 1) & (u < U - 3))
        def _():
            choose(u // 3 + 1)

    def add_pair(u):
        pair_copy(u).wait_recv()

        def total(chip):
            rows = pl.ds(pl.multiple_of(chip * R, R), R)
            return part_own[u % (to_pair + 1), rows, :] + pair_recv[u, rows, :].astype(F32)

        if grid:
            y = total(C - 1 - c)
            for n in range(2):
                half_send[u, n] = y[:, n * H : (n + 1) * H].astype(BF16)
                half_copy(u, n).start()
            for n in range(2):
                held[u % (to_half - to_pair + 1), n] = total(across[n])
        else:
            for n in range(pieces):
                rs_send[u, n] = total(lax.rem(c + n + 1, C)).astype(BF16)
                rs_copy(u, n).start()
        proj_own[u] = total(c)

    def add_half(u):
        if grid:
            for n in range(2):
                half_copy(u, 1 - n).wait_recv()
                near, other = slice((1 - n) * H, (2 - n) * H), slice(n * H, (n + 1) * H)
                rs_send[u, n, :, near] = (held[u % (to_half - to_pair + 1), n, :, near] + half_recv[u, 1 - n].astype(F32)).astype(BF16)
                rs_send[u, n, :, other] = held[u % (to_half - to_pair + 1), n, :, other].astype(BF16)
                rs_copy(u, n).start()

    def receive(u):
        rows = pl.ds(pl.multiple_of((u // 3) * R, R), R)
        for n in range(pieces):
            rs_copy(u, n).wait_recv()
        y = proj_own[u]
        for n in range(pieces):
            y = y + rs_recv[u, n].astype(F32)
        heads = [slice(h * HS, (h + 1) * HS) for h in range(HL)]

        @pl.when(u % 3 == 0)
        def _():
            for cols in heads:
                k_ref[rows, cols] = row_norm(y[:, cols], kgain_ref[...]).astype(BF16)

        @pl.when(u % 3 == 1)
        def _():
            v_ref[rows, :] = y.astype(BF16)

        @pl.when(u % 3 == 2)
        def _():
            for cols in heads:
                q_ref[rows, cols] = row_norm(y[:, cols], qgain_ref[...]).astype(BF16)

    inner = ((z + 1) // 2) % 2
    last = z // 3

    def out_copy(a, k):
        rows = pl.ds(pl.multiple_of(a * R, R), R)
        return remote(
            out_send.at[k, rows], out_recv.at[k, rows], out_s.at[k, a], out_r.at[k, a], (d, lax.rem(z + k, Z))
        )

    def end_copy(a, k):
        rows = pl.ds(pl.multiple_of(a * R, R), R)
        return remote(out_send.at[k, rows], end_recv.at[rows], out_s.at[k, a], end_r.at[a], (d, 1 + last))

    def attend(a):
        rows = pl.ds(pl.multiple_of(a * R, R), R)
        same_image = mask_ref[rows, :] > 0.5
        heads = [slice(h * HS, (h + 1) * HS) for h in range(HL)]
        scores = [
            lax.dot_general(
                q_ref[rows, cols], k_ref[:, cols], (((1,), (1,)), ((), ())), preferred_element_type=F32
            )
            for cols in heads
        ]
        raw = [jnp.where(same_image, jnp.exp(s * HS ** (-0.5)), 0.0) for s in scores]
        totals = [jnp.sum(w, axis=-1, keepdims=True) for w in raw]
        attention = [(w / total).astype(BF16) for w, total in zip(raw, totals)]
        terms = [
            jnp.dot(w, v_ref[:, cols], preferred_element_type=F32).astype(BF16) for w, cols in zip(attention, heads)
        ]
        for term, cols in zip(terms, heads):
            context[:, cols] = term
        for t in range(Z):
            if t == Z - 1:
                k = 0
            elif relayed:
                k = inner * (1, 3, 2)[t] + (1 - inner) * ((1 - last) * (3 - t) + last * (1 + t))
            else:
                k = t + 1
            m = lax.rem(z + k, Z)
            y = jnp.dot(context[...], w_out[m], preferred_element_type=F32).astype(BF16)
            if t == Z - 1:
                out_own[rows, :] = y
            else:
                out_send[k, rows, :] = y
                if not relayed or t == 1:
                    out_copy(a, k).start()
                elif t == 0:

                    @pl.when(inner == 0)
                    def _():
                        end_copy(a, k).start()

                    @pl.when(inner == 1)
                    def _():
                        out_copy(a, k).start()

                else:

                    @pl.when(inner == 0)
                    def _():
                        out_copy(a, k).start()

    def pass_on(a):
        if relayed:

            @pl.when(inner == 1)
            def _():
                rows = pl.ds(pl.multiple_of(a * R, R), R)
                end_copy(a, 2).wait_recv()
                out_send[2, rows, :] = (
                    out_send[2, rows, :].astype(F32) + end_recv[rows, :].astype(F32)
                ).astype(BF16)
                out_copy(a, 2).start()

    for cp in out_loads:
        cp.wait()

    @pl.loop(0, U + to_take)
    def _(v):
        @pl.when(v < U)
        def _():
            project(v)

        @pl.when((v >= to_pair) & (v < U + to_pair))
        def _():
            add_pair(v - to_pair)

        @pl.when((v >= to_half) & (v < U + to_half))
        def _():
            add_half(v - to_half)

        @pl.when(v >= to_take)
        def _():
            u = v - to_take
            receive(u)

            @pl.when((u >= 7) & (u % 3 == 1))
            def _():
                pass_on((u - 7) // 3)

            @pl.when((u >= 4) & (u % 3 == 1))
            def _():
                attend((u - 4) // 3)

    attend(NCH - 1)
    pass_on(NCH - 2)
    pass_on(NCH - 1)

    for i in range(SUB):
        for k in range(1, Z):

            @pl.when(own_goes(k))
            def _():
                own_copy(k, i).wait_send()

        if relayed:

            @pl.when(middle)
            def _():
                relay_copy(i).wait_send()

        for m in range(Z):
            for h in range(2):

                @pl.when(2 * m + h != d)
                def _():
                    norm_copy(m, h, i).wait_send()

    @pl.loop(0, U)
    def _(u):
        pair_copy(u).wait_send()
        for n in range(pieces):
            rs_copy(u, n).wait_send()
        if grid:
            for n in range(2):
                half_copy(u, n).wait_send()

    stores = []
    for a in range(NCH):
        rows = slice(a * R, (a + 1) * R)
        y = out_own[rows, :].astype(F32)
        for k in range(1, Z):
            out_copy(a, k).wait_send()
            if relayed and k != 2:
                direct = jnp.abs(lax.rem(z + Z - k, Z) - z) < 3

                @pl.when(direct)
                def _():
                    out_copy(a, k).wait_recv()

                y = y + jnp.where(direct, out_recv[k, rows, :].astype(F32), 0.0)
            else:
                out_copy(a, k).wait_recv()
                y = y + out_recv[k, rows, :].astype(F32)
        attended_v[rows, :] = y.astype(BF16)
        stores.append(pltpu.make_async_copy(attended_v.at[rows], attended_hbm.at[rows], store_sem.at[1 + a]))
        stores[a].start()
    packed_store.wait()
    for store in stores:
        store.wait()


def hand_over(packed_in, attended_in, packed_out, attended_out):
    packed_out[...] = packed_in[...]
    attended_out[...] = attended_in[...]


def on_device(
    n_dp, Z, patches, send_start, run_length, slot_start, image_ids, norm_gain, qkv_weight, query_gain, key_gain, out_weight
):
    T, FL = patches.shape
    KS, _, NH = qkv_weight.shape
    HS = query_gain.shape[0]
    C = n_dp // 2
    R, SUB = 32, 4
    NCH = T // R
    U, pieces = 3 * NCH, 2 if C == 4 else C - 1
    cap = max(16, 2 * T // n_dp)
    dims = (n_dp, Z, T, FL, KS, NH, HS, R, SUB, cap)
    dma = pltpu.SemaphoreType.DMA
    vmem = pltpu.VMEM
    scratch = [
        vmem((Z, T, FL), BF16),
        vmem((Z, 2, T, KS), BF16),
        vmem((n_dp, T, KS), BF16),
        vmem((3, KS, NH), BF16),
        vmem((Z, NH, FL), BF16),
        vmem((Z, 8, 128), F32),
        vmem((T, 128), F32),
        vmem((T, 128), F32),
        vmem((128, 128), F32),
        vmem((n_dp, 8, 128), I32),
        vmem((n_dp, T), I32),
        vmem((n_dp * cap, T), BF16),
        vmem((n_dp, cap, FL), BF16),
        vmem((n_dp, cap, FL), BF16),
        vmem((T, n_dp * cap), BF16),
        vmem((T, FL), BF16),
        vmem((2 * C * R, n_dp * T), BF16),
        vmem((2 * C * R, KS), BF16),
        vmem((U, C * R, NH), BF16),
        vmem((U, C * R, NH), BF16),
        vmem((to_pair + 1, C * R, NH), F32),
        vmem((U, 2, R, NH // 2), BF16),
        vmem((U, 2, R, NH // 2), BF16),
        vmem((to_half - to_pair + 1, 2, R, NH), F32),
        vmem((U, pieces, R, NH), BF16),
        vmem((U, pieces, R, NH), BF16),
        vmem((U, R, NH), F32),
        vmem((T, NH), BF16),
        vmem((T, NH), BF16),
        vmem((T, NH), BF16),
        vmem((T, T), F32),
        vmem((R, NH), BF16),
        vmem((Z, T, FL), BF16),
        vmem((Z, T, FL), BF16),
        vmem((T, FL), BF16),
        vmem((T, FL), BF16),
        vmem((T, FL), BF16),
        dma,
        dma((1 + Z,)),
        dma((1 + NCH,)),
        dma((Z,)), dma((Z,)),
        dma((n_dp,)), dma((n_dp,)),
        dma((n_dp,)), dma((n_dp,)),
        dma((Z, SUB)), dma((Z, SUB)), dma((SUB,)),
        dma((Z, 2, SUB)), dma((n_dp, SUB)),
        dma((U,)), dma((U,)),
        dma((U, 2)), dma((U, 2)),
        dma((U, pieces)), dma((U, pieces)),
        dma((Z, NCH)), dma((Z, NCH)), dma((NCH,)),
    ]
    in_vmem = pl.BlockSpec(memory_space=pltpu.VMEM)
    anywhere = pl.BlockSpec(memory_space=pl.ANY)
    outs = pl.pallas_call(
        functools.partial(kernel, dims),
        out_shape=(jax.ShapeDtypeStruct((T, FL), BF16),) * 2,
        in_specs=[anywhere] + [in_vmem] * 5 + [anywhere] + [in_vmem] * 2 + [anywhere],
        out_specs=(anywhere,) * 2,
        scratch_shapes=scratch,
        compiler_params=pltpu.CompilerParams(
            collective_id=0, has_side_effects=True, vmem_limit_bytes=60 * 1024 * 1024
        ),
    )(
        patches, send_start, run_length, slot_start, image_ids, norm_gain.reshape(1, -1),
        jnp.transpose(qkv_weight, (1, 0, 2)), query_gain.reshape(1, -1), key_gain.reshape(1, -1), out_weight,
    )
    return tuple(
        pl.pallas_call(
            hand_over, out_shape=(jax.ShapeDtypeStruct((T, FL), BF16),) * 2, in_specs=[in_vmem] * 2, out_specs=(in_vmem,) * 2
        )(*outs)
    )


def solution(mesh):
    n_dp, Z = mesh.shape["dp"], mesh.shape["mp"]
    assert n_dp == 2 * Z
    return jax.shard_map(
        functools.partial(on_device, n_dp, Z),
        mesh=mesh,
        in_specs=(
            P("dp", "mp"),
            P("dp", None),
            P("dp", None),
            P("dp", None),
            P("dp", None),
            P(),
            P("dp", None, "mp"),
            P(),
            P(),
            P("mp", None),
        ),
        out_specs=(P("dp", "mp"), P("dp", "mp")),
        check_vma=False,
    )
```

```python
import functools

import jax
import jax.numpy as jnp
from jax import lax
from jax.experimental import pallas as pl
from jax.experimental.pallas import tpu as pltpu
from jax.sharding import PartitionSpec as P

MESH = pl.DeviceIdType.MESH
F32, BF16, I32 = jnp.float32, jnp.bfloat16, jnp.int32
epsilon = 1e-06
to_pair, to_half, to_take = 2, 4, 7


def row_norm(values, scales):
    middle = jnp.mean(values, axis=-1, keepdims=True)
    spread = jnp.mean(values * values, axis=-1, keepdims=True) - middle * middle
    return (values - middle) * lax.rsqrt(spread + epsilon) * scales


def remote(src, dst, send_sem, recv_sem, target):
    return pltpu.make_async_remote_copy(
        src_ref=src, dst_ref=dst, send_sem=send_sem, recv_sem=recv_sem, device_id=target, device_id_type=MESH
    )


def kernel(
    dims,
    patches_hbm, start_ref, length_ref, slot_ref, image_ref, gain_ref, wqkv_hbm, qgain_ref, kgain_ref, wout_hbm,
    packed_hbm, attended_hbm,
    blocks, normed, gathered, w_qkv, w_out, stats, mean_col, rstd_col, square, tables, dest_ref,
    pick_ref, run_send, run_recv, place_ref, packed_v,
    chosen, ordered, pair_send, pair_recv, part_own, half_send, half_recv, held, rs_send, rs_recv, proj_own,
    q_ref, k_ref, v_ref, mask_ref, context, out_send, out_recv, end_recv, out_own, attended_v,
    load_sem, wload_sem, store_sem, stat_s, stat_r, tab_s, tab_r, run_s, run_r,
    block_s, block_r, relay_s, norm_s, norm_r, pair_s, pair_r, half_s, half_r, rs_s, rs_r, out_s, out_r, end_r,
):
    n_dp, Z, T, FL, KS, NH, HS, R, SUB, cap = dims
    C = n_dp // 2
    HL = NH // HS
    NCH = T // R
    SR = T // SUB
    D = FL * Z
    NT = min(1024, NH)
    d, z = lax.axis_index("dp"), lax.axis_index("mp")
    c, j = d // 2, d % 2
    sibling = (d + 1 - 2 * j, z)

    load = pltpu.make_async_copy(patches_hbm, blocks.at[z], load_sem)
    load.start()
    barrier = pltpu.get_barrier_semaphore()
    for k in range(1, n_dp):
        pl.semaphore_signal(barrier, inc=1, device_id=(lax.rem(d + k, n_dp), z), device_id_type=MESH)
    for k in range(1, Z):
        pl.semaphore_signal(barrier, inc=1, device_id=(d, lax.rem(z + k, Z)), device_id_type=MESH)

    def stat_copy(k):
        return remote(stats.at[z], stats.at[z], stat_s.at[k], stat_r.at[k], (d, lax.rem(z + k, Z)))

    relayed = Z == 4

    def block_copy(m, i, target, send_sem):
        block = blocks.at[m, pl.ds(i * SR, SR)]
        return remote(block, block, send_sem, block_r.at[m, i], (d, target))

    def own_copy(k, i):
        rows = pl.ds(i * SR, SR)
        return remote(
            patches_hbm.at[rows], blocks.at[z, rows], block_s.at[k, i], block_r.at[z, i], (d, lax.rem(z + k, Z))
        )

    def own_goes(k):
        t = lax.rem(z + k, Z)
        return jnp.abs(t - z) < 3 if relayed else t >= 0

    def relay_copy(i):
        return block_copy(lax.rem(z + 2, Z), i, 3 * (z - 1), relay_s.at[i])

    middle = (z >= 1) & (z <= 2)

    def tab_copy(k):
        return remote(tables.at[d], tables.at[d], tab_s.at[k], tab_r.at[k], (lax.rem(d + k, n_dp), z))

    def run_copy(k):
        t = lax.rem(d + k, n_dp)
        return remote(run_send.at[t], run_recv.at[d], run_s.at[k], run_r.at[k], (t, z))

    pl.semaphore_wait(barrier, n_dp - 1 + Z - 1)
    def start_own(i):
        for k in sorted(range(1, Z), key=lambda k: abs(k - Z // 2)):

            @pl.when(own_goes(k))
            def _():
                own_copy(k, i).start()

    start_own(0)
    tables[d] = jnp.zeros((8, 128), I32)
    tables[d, 0:1, 0:n_dp] = start_ref[...]
    tables[d, 1:2, 0:n_dp] = length_ref[...]
    tables[d, 2:3, 0:n_dp] = slot_ref[...]
    load.wait()
    weight_load = pltpu.make_async_copy(wqkv_hbm, w_qkv, wload_sem.at[0])
    weight_load.start()
    out_loads = [
        pltpu.make_async_copy(wout_hbm.at[:, pl.ds(m * FL, FL)], w_out.at[m], wload_sem.at[1 + m]) for m in range(Z)
    ]
    for cp in out_loads:
        cp.start()
    x = blocks[z].astype(F32)
    stats[z] = jnp.zeros((8, 128), F32)
    stats[z, 0:1, :] = jnp.broadcast_to(jnp.sum(x, axis=-1, keepdims=True), (T, 128)).T[0:1, :]
    stats[z, 1:2, :] = jnp.broadcast_to(jnp.sum(x * x, axis=-1, keepdims=True), (T, 128)).T[0:1, :]
    for k in range(1, Z):
        stat_copy(k).start()
    for i in range(1, SUB):
        start_own(i)
    for k in range(1, n_dp):
        tab_copy(k).start()

    within = lax.broadcasted_iota(I32, (cap, T), 0)
    lane = lax.broadcasted_iota(I32, (cap, T), 1)
    for p in range(n_dp):
        hit = (within + start_ref[0:1, p : p + 1] == lane) & (within < length_ref[0:1, p : p + 1])
        pick_ref[p * cap : (p + 1) * cap, :] = hit.astype(F32).astype(BF16)
    run_send[...] = (
        jnp.dot(pick_ref[...], blocks[z], preferred_element_type=F32).astype(BF16).reshape(n_dp, cap, FL)
    )
    run_recv[d] = run_send[d]
    for k in range(1, n_dp):
        run_copy(k).start()

    for k in range(1, Z):
        stat_copy(k).wait()
    total = jnp.sum(stats[...], axis=0) * (1.0 / D)
    mean_row = total[0:1, :]
    rstd_row = lax.rsqrt(total[1:2, :] - mean_row * mean_row + epsilon)
    mean_col[...] = jnp.broadcast_to(mean_row, (T, 128)).T
    rstd_col[...] = jnp.broadcast_to(rstd_row, (T, 128)).T

    def norm_copy(m, h, i):
        rows = pl.ds(i * SR, SR)
        return remote(
            normed.at[m, h, rows], gathered.at[d, rows], norm_s.at[m, h, i], norm_r.at[d, i], (2 * m + h, z)
        )

    def spread(m, i):
        rows = pl.ds(i * SR, SR)
        gain = gain_ref[:, pl.ds(pl.multiple_of(m * FL, 128), FL)]
        raw = blocks[m, rows, :].astype(F32)
        done = ((raw - mean_col[rows, 0:1]) * rstd_col[rows, 0:1] * gain).astype(BF16)
        for h in range(2):
            normed[m, h, rows, :] = done[:, h * KS : (h + 1) * KS]

            @pl.when(2 * m + h != d)
            def _():
                norm_copy(m, h, i).start()

            @pl.when(2 * m + h == d)
            def _():
                gathered[d, rows, :] = normed[m, h, rows, :]

    def destinations():
        for k in range(1, n_dp):
            tab_copy(k).wait()
        starts, lengths = tables[:, 0, :], tables[:, 1, :]
        square[...] = jnp.zeros((128, 128), F32)
        square[0:n_dp, :] = tables[:, 2, :].astype(F32)
        slots = square[...].T[0:n_dp, :].astype(I32)
        u = lax.broadcasted_iota(I32, (n_dp, T), 1)
        dest = jnp.zeros((n_dp, T), I32)
        for p in range(n_dp):
            first = starts[:, p : p + 1]
            inside = (u >= first) & (u < first + lengths[:, p : p + 1])
            dest = dest + jnp.where(inside, u + (slots[:, p : p + 1] - first + p * T), 0)
        dest_ref[...] = dest

        same = jnp.broadcast_to(image_ref[...].astype(F32), (T, T))
        mask_ref[...] = (same == same.T).astype(F32)
        k_ref[...] = jnp.zeros_like(k_ref)
        v_ref[...] = jnp.zeros_like(v_ref)

    def place_runs():
        for k in range(1, n_dp):
            run_copy(k).wait()
        spot = lax.broadcasted_iota(I32, (1, n_dp * cap), 1)
        goal = spot % cap
        for s in range(n_dp):
            goal = goal + jnp.where(spot // cap == s, slot_ref[0:1, s : s + 1], 0)
        place_ref[...] = (lax.broadcasted_iota(I32, (T, n_dp * cap), 0) == goal).astype(F32).astype(BF16)
        packed_v[...] = jnp.dot(
            place_ref[...], run_recv[...].reshape(n_dp * cap, FL), preferred_element_type=F32
        ).astype(BF16)
        packed_store.start()

    packed_store = pltpu.make_async_copy(packed_v, packed_hbm, store_sem.at[0])

    def take(m, i):
        block_copy(m, i, z, relay_s.at[i]).wait_recv()

    for i in range(SUB):
        spread(z, i)
        if i == 1:
            destinations()
        if i == 2:
            place_runs()
        for s in [2, 1] + list(range(3, Z)):
            for m in (z - s, z + s):

                @pl.when((m >= 0) & (m < Z))
                def _():
                    take(m, i)

                    if relayed and s == 2:

                        @pl.when(middle)
                        def _():
                            relay_copy(i).start()

                    spread(m, i)

    CR = C * R

    def choose(r):
        row = lax.broadcasted_iota(I32, (2 * CR, T), 0)
        side = row // CR
        row = row % CR
        goal = (row // R) * (2 * T) + row % R + r * R + T * (side * j + (1 - side) * (1 - j))
        for s in range(n_dp):
            chosen[:, s * T : (s + 1) * T] = (dest_ref[s : s + 1, :] == goal).astype(F32).astype(BF16)

    choose(0)

    def wait_gathered(k, i):
        t = lax.rem(d + k, n_dp)
        rows = pl.ds(i * SR, SR)
        remote(normed.at[0, 0, rows], gathered.at[t, rows], norm_s.at[0, 0, i], norm_r.at[t, i], (t, z)).wait_recv()

    for i in range(SUB):

        @pl.loop(1, n_dp)
        def _(k):
            wait_gathered(k, i)

    U = 3 * NCH
    H = NH // 2
    grid = C == 4
    across = c + 1 - 2 * (c % 2), c + 2 - 4 * (c // 2)
    weight_load.wait()

    def pair_copy(u):
        return remote(pair_send.at[u], pair_recv.at[u], pair_s.at[u], pair_r.at[u], sibling)

    def half_copy(u, n):
        return remote(half_send.at[u, n], half_recv.at[u, n], half_s.at[u, n], half_r.at[u, n], (2 * across[n] + j, z))

    def rs_copy(u, n):
        chip = across[n] if grid else lax.rem(c + n + 1, C)
        return remote(rs_send.at[u, n], rs_recv.at[u, n], rs_s.at[u, n], rs_r.at[u, n], (2 * chip + j, z))

    pieces = 2 if grid else C - 1

    def project(u):
        @pl.when(u % 3 == 0)
        def _():
            ordered[...] = jnp.dot(
                chosen[...], gathered[...].reshape(n_dp * T, KS), preferred_element_type=F32
            ).astype(BF16)

        @pl.loop(0, NH // NT)
        def _(n):
            cols = pl.ds(pl.multiple_of(n * NT, 128), NT)
            y = jnp.dot(ordered[...], w_qkv[(u + 1) % 3, :, cols], preferred_element_type=F32)
            pair_send[u, :, cols] = y[:CR].astype(BF16)
            part_own[u % (to_pair + 1), :, cols] = y[CR:]

        pair_copy(u).start()

        @pl.when((u % 3 == 1) & (u < U - 3))
        def _():
            choose(u // 3 + 1)

    def add_pair(u):
        pair_copy(u).wait_recv()

        def total(chip):
            rows = pl.ds(pl.multiple_of(chip * R, R), R)
            return part_own[u % (to_pair + 1), rows, :] + pair_recv[u, rows, :].astype(F32)

        if grid:
            y = total(C - 1 - c)
            for n in range(2):
                half_send[u, n] = y[:, n * H : (n + 1) * H].astype(BF16)
                half_copy(u, n).start()
            for n in range(2):
                held[u % (to_half - to_pair + 1), n] = total(across[n])
        else:
            for n in range(pieces):
                rs_send[u, n] = total(lax.rem(c + n + 1, C)).astype(BF16)
                rs_copy(u, n).start()
        proj_own[u] = total(c)

    def add_half(u):
        if grid:
            for n in range(2):
                half_copy(u, 1 - n).wait_recv()
                near, other = slice((1 - n) * H, (2 - n) * H), slice(n * H, (n + 1) * H)
                rs_send[u, n, :, near] = (held[u % (to_half - to_pair + 1), n, :, near] + half_recv[u, 1 - n].astype(F32)).astype(BF16)
                rs_send[u, n, :, other] = held[u % (to_half - to_pair + 1), n, :, other].astype(BF16)
                rs_copy(u, n).start()

    def receive(u):
        rows = pl.ds(pl.multiple_of((u // 3) * R, R), R)
        for n in range(pieces):
            rs_copy(u, n).wait_recv()
        y = proj_own[u]
        for n in range(pieces):
            y = y + rs_recv[u, n].astype(F32)
        heads = [slice(h * HS, (h + 1) * HS) for h in range(HL)]

        @pl.when(u % 3 == 0)
        def _():
            for cols in heads:
                k_ref[rows, cols] = row_norm(y[:, cols], kgain_ref[...]).astype(BF16)

        @pl.when(u % 3 == 1)
        def _():
            v_ref[rows, :] = y.astype(BF16)

        @pl.when(u % 3 == 2)
        def _():
            for cols in heads:
                q_ref[rows, cols] = row_norm(y[:, cols], qgain_ref[...]).astype(BF16)

    inner = ((z + 1) // 2) % 2
    last = z // 3

    def out_copy(a, k):
        rows = pl.ds(pl.multiple_of(a * R, R), R)
        return remote(
            out_send.at[k, rows], out_recv.at[k, rows], out_s.at[k, a], out_r.at[k, a], (d, lax.rem(z + k, Z))
        )

    def end_copy(a, k):
        rows = pl.ds(pl.multiple_of(a * R, R), R)
        return remote(out_send.at[k, rows], end_recv.at[rows], out_s.at[k, a], end_r.at[a], (d, 1 + last))

    def attend(a):
        rows = pl.ds(pl.multiple_of(a * R, R), R)
        same_image = mask_ref[rows, :] > 0.5
        heads = [slice(h * HS, (h + 1) * HS) for h in range(HL)]
        scores = [
            lax.dot_general(
                q_ref[rows, cols], k_ref[:, cols], (((1,), (1,)), ((), ())), preferred_element_type=F32
            )
            for cols in heads
        ]
        raw = [jnp.where(same_image, jnp.exp(s * HS ** (-0.5)), 0.0) for s in scores]
        totals = [jnp.sum(w, axis=-1, keepdims=True) for w in raw]
        attention = [(w / total).astype(BF16) for w, total in zip(raw, totals)]
        terms = [
            jnp.dot(w, v_ref[:, cols], preferred_element_type=F32).astype(BF16) for w, cols in zip(attention, heads)
        ]
        for term, cols in zip(terms, heads):
            context[:, cols] = term
        for t in range(Z):
            if t == Z - 1:
                k = 0
            elif relayed:
                k = inner * (1, 3, 2)[t] + (1 - inner) * ((1 - last) * (3 - t) + last * (1 + t))
            else:
                k = t + 1
            m = lax.rem(z + k, Z)
            y = jnp.dot(context[...], w_out[m], preferred_element_type=F32).astype(BF16)
            if t == Z - 1:
                out_own[rows, :] = y
            else:
                out_send[k, rows, :] = y
                if not relayed or t == 1:
                    out_copy(a, k).start()
                elif t == 0:

                    @pl.when(inner == 0)
                    def _():
                        end_copy(a, k).start()

                    @pl.when(inner == 1)
                    def _():
                        out_copy(a, k).start()

                else:

                    @pl.when(inner == 0)
                    def _():
                        out_copy(a, k).start()

    def pass_on(a):
        if relayed:

            @pl.when(inner == 1)
            def _():
                rows = pl.ds(pl.multiple_of(a * R, R), R)
                end_copy(a, 2).wait_recv()
                out_send[2, rows, :] = (
                    out_send[2, rows, :].astype(F32) + end_recv[rows, :].astype(F32)
                ).astype(BF16)
                out_copy(a, 2).start()

    for cp in out_loads:
        cp.wait()

    @pl.loop(0, U + to_take)
    def _(v):
        @pl.when(v < U)
        def _():
            project(v)

        @pl.when((v >= to_pair) & (v < U + to_pair))
        def _():
            add_pair(v - to_pair)

        @pl.when((v >= to_half) & (v < U + to_half))
        def _():
            add_half(v - to_half)

        @pl.when(v >= to_take)
        def _():
            u = v - to_take
            receive(u)

            @pl.when((u >= 7) & (u % 3 == 1))
            def _():
                pass_on((u - 7) // 3)

            @pl.when((u >= 4) & (u % 3 == 1))
            def _():
                attend((u - 4) // 3)

    attend(NCH - 1)
    pass_on(NCH - 2)
    pass_on(NCH - 1)

    for i in range(SUB):
        for k in range(1, Z):

            @pl.when(own_goes(k))
            def _():
                own_copy(k, i).wait_send()

        if relayed:

            @pl.when(middle)
            def _():
                relay_copy(i).wait_send()

        for m in range(Z):
            for h in range(2):

                @pl.when(2 * m + h != d)
                def _():
                    norm_copy(m, h, i).wait_send()

    @pl.loop(0, U)
    def _(u):
        pair_copy(u).wait_send()
        for n in range(pieces):
            rs_copy(u, n).wait_send()
        if grid:
            for n in range(2):
                half_copy(u, n).wait_send()

    stores = []
    for a in range(NCH):
        rows = slice(a * R, (a + 1) * R)
        y = out_own[rows, :].astype(F32)
        for k in range(1, Z):
            out_copy(a, k).wait_send()
            if relayed and k != 2:
                direct = jnp.abs(lax.rem(z + Z - k, Z) - z) < 3

                @pl.when(direct)
                def _():
                    out_copy(a, k).wait_recv()

                y = y + jnp.where(direct, out_recv[k, rows, :].astype(F32), 0.0)
            else:
                out_copy(a, k).wait_recv()
                y = y + out_recv[k, rows, :].astype(F32)
        attended_v[rows, :] = y.astype(BF16)
        stores.append(pltpu.make_async_copy(attended_v.at[rows], attended_hbm.at[rows], store_sem.at[1 + a]))
        stores[a].start()
    packed_store.wait()
    for store in stores:
        store.wait()


def hand_over(packed_in, attended_in, packed_out, attended_out, held, load_sem, store_sem):
    piece = held.shape[2]
    loads, stores = [], []
    for n, (source, goal) in enumerate(((packed_in, packed_out), (attended_in, attended_out))):
        for i in range(held.shape[1]):
            rows = pl.ds(i * piece, piece)
            loads.append(pltpu.make_async_copy(source.at[rows], held.at[n, i], load_sem.at[n, i]))
            stores.append(pltpu.make_async_copy(held.at[n, i], goal.at[rows], store_sem.at[n, i]))
    for load in loads:
        load.start()
    for load, store in zip(loads, stores):
        load.wait()
        store.start()
    for store in stores:
        store.wait()


def on_device(
    n_dp, Z, patches, send_start, run_length, slot_start, image_ids, norm_gain, qkv_weight, query_gain, key_gain, out_weight
):
    T, FL = patches.shape
    KS, _, NH = qkv_weight.shape
    HS = query_gain.shape[0]
    C = n_dp // 2
    R, SUB = 32, 4
    NCH = T // R
    U, pieces = 3 * NCH, 2 if C == 4 else C - 1
    cap = max(16, 2 * T // n_dp)
    dims = (n_dp, Z, T, FL, KS, NH, HS, R, SUB, cap)
    dma = pltpu.SemaphoreType.DMA
    vmem = pltpu.VMEM
    scratch = [
        vmem((Z, T, FL), BF16),
        vmem((Z, 2, T, KS), BF16),
        vmem((n_dp, T, KS), BF16),
        vmem((3, KS, NH), BF16),
        vmem((Z, NH, FL), BF16),
        vmem((Z, 8, 128), F32),
        vmem((T, 128), F32),
        vmem((T, 128), F32),
        vmem((128, 128), F32),
        vmem((n_dp, 8, 128), I32),
        vmem((n_dp, T), I32),
        vmem((n_dp * cap, T), BF16),
        vmem((n_dp, cap, FL), BF16),
        vmem((n_dp, cap, FL), BF16),
        vmem((T, n_dp * cap), BF16),
        vmem((T, FL), BF16),
        vmem((2 * C * R, n_dp * T), BF16),
        vmem((2 * C * R, KS), BF16),
        vmem((U, C * R, NH), BF16),
        vmem((U, C * R, NH), BF16),
        vmem((to_pair + 1, C * R, NH), F32),
        vmem((U, 2, R, NH // 2), BF16),
        vmem((U, 2, R, NH // 2), BF16),
        vmem((to_half - to_pair + 1, 2, R, NH), F32),
        vmem((U, pieces, R, NH), BF16),
        vmem((U, pieces, R, NH), BF16),
        vmem((U, R, NH), F32),
        vmem((T, NH), BF16),
        vmem((T, NH), BF16),
        vmem((T, NH), BF16),
        vmem((T, T), F32),
        vmem((R, NH), BF16),
        vmem((Z, T, FL), BF16),
        vmem((Z, T, FL), BF16),
        vmem((T, FL), BF16),
        vmem((T, FL), BF16),
        vmem((T, FL), BF16),
        dma,
        dma((1 + Z,)),
        dma((1 + NCH,)),
        dma((Z,)), dma((Z,)),
        dma((n_dp,)), dma((n_dp,)),
        dma((n_dp,)), dma((n_dp,)),
        dma((Z, SUB)), dma((Z, SUB)), dma((SUB,)),
        dma((Z, 2, SUB)), dma((n_dp, SUB)),
        dma((U,)), dma((U,)),
        dma((U, 2)), dma((U, 2)),
        dma((U, pieces)), dma((U, pieces)),
        dma((Z, NCH)), dma((Z, NCH)), dma((NCH,)),
    ]
    in_vmem = pl.BlockSpec(memory_space=pltpu.VMEM)
    anywhere = pl.BlockSpec(memory_space=pl.ANY)
    outs = pl.pallas_call(
        functools.partial(kernel, dims),
        out_shape=(jax.ShapeDtypeStruct((T, FL), BF16),) * 2,
        in_specs=[anywhere] + [in_vmem] * 5 + [anywhere] + [in_vmem] * 2 + [anywhere],
        out_specs=(anywhere,) * 2,
        scratch_shapes=scratch,
        compiler_params=pltpu.CompilerParams(
            collective_id=0, has_side_effects=True, vmem_limit_bytes=60 * 1024 * 1024
        ),
    )(
        patches, send_start, run_length, slot_start, image_ids, norm_gain.reshape(1, -1),
        jnp.transpose(qkv_weight, (1, 0, 2)), query_gain.reshape(1, -1), key_gain.reshape(1, -1), out_weight,
    )
    return tuple(
        pl.pallas_call(
            hand_over,
            out_shape=(jax.ShapeDtypeStruct((T, FL), BF16),) * 2,
            in_specs=[anywhere] * 2,
            out_specs=(anywhere,) * 2,
            scratch_shapes=[vmem((2, 2, T // 2, FL), BF16), dma((2, 2)), dma((2, 2))],
        )(*outs)
    )


def solution(mesh):
    n_dp, Z = mesh.shape["dp"], mesh.shape["mp"]
    assert n_dp == 2 * Z
    return jax.shard_map(
        functools.partial(on_device, n_dp, Z),
        mesh=mesh,
        in_specs=(
            P("dp", "mp"),
            P("dp", None),
            P("dp", None),
            P("dp", None),
            P("dp", None),
            P(),
            P("dp", None, "mp"),
            P(),
            P(),
            P("mp", None),
        ),
        out_specs=(P("dp", "mp"), P("dp", "mp")),
        check_vma=False,
    )
```

```python
import functools

import jax
import jax.numpy as jnp
from jax import lax
from jax.experimental import pallas as pl
from jax.experimental.pallas import tpu as pltpu
from jax.sharding import PartitionSpec as P

MESH = pl.DeviceIdType.MESH
F32, BF16, I32 = jnp.float32, jnp.bfloat16, jnp.int32
epsilon = 1e-06
to_pair, to_half, to_take = 2, 4, 7


def row_norm(values, scales):
    middle = jnp.mean(values, axis=-1, keepdims=True)
    spread = jnp.mean(values * values, axis=-1, keepdims=True) - middle * middle
    return (values - middle) * lax.rsqrt(spread + epsilon) * scales


def remote(src, dst, send_sem, recv_sem, target):
    return pltpu.make_async_remote_copy(
        src_ref=src, dst_ref=dst, send_sem=send_sem, recv_sem=recv_sem, device_id=target, device_id_type=MESH
    )


def kernel(
    dims,
    patches_hbm, start_ref, length_ref, slot_ref, image_ref, gain_ref, wqkv_hbm, qgain_ref, kgain_ref, wout_hbm,
    packed_hbm, attended_hbm,
    blocks, normed, gathered, w_qkv, w_out, stats, mean_col, rstd_col, square, tables, dest_ref,
    pick_ref, run_send, run_recv, place_ref, packed_v,
    chosen, ordered, pair_send, pair_recv, part_own, half_send, half_recv, held, rs_send, rs_recv, proj_own,
    q_ref, k_ref, v_ref, mask_ref, context, out_send, out_recv, end_recv, out_own, attended_v,
    load_sem, wload_sem, store_sem, stat_s, stat_r, tab_s, tab_r, run_s, run_r,
    block_s, block_r, relay_s, norm_s, norm_r, pair_s, pair_r, half_s, half_r, rs_s, rs_r, out_s, out_r, end_r,
):
    n_dp, Z, T, FL, KS, NH, HS, R, SUB, cap = dims
    C = n_dp // 2
    HL = NH // HS
    NCH = T // R
    SR = T // SUB
    D = FL * Z
    NT = min(1024, NH)
    d, z = lax.axis_index("dp"), lax.axis_index("mp")
    c, j = d // 2, d % 2
    sibling = (d + 1 - 2 * j, z)

    load = pltpu.make_async_copy(patches_hbm, blocks.at[z], load_sem)
    load.start()
    barrier = pltpu.get_barrier_semaphore()
    for k in range(1, n_dp):
        pl.semaphore_signal(barrier, inc=1, device_id=(lax.rem(d + k, n_dp), z), device_id_type=MESH)
    for k in range(1, Z):
        pl.semaphore_signal(barrier, inc=1, device_id=(d, lax.rem(z + k, Z)), device_id_type=MESH)

    def stat_copy(k):
        return remote(stats.at[z], stats.at[z], stat_s.at[k], stat_r.at[k], (d, lax.rem(z + k, Z)))

    relayed = Z == 4

    def block_copy(m, i, target, send_sem):
        block = blocks.at[m, pl.ds(i * SR, SR)]
        return remote(block, block, send_sem, block_r.at[m, i], (d, target))

    def own_copy(k, i):
        rows = pl.ds(i * SR, SR)
        return remote(
            patches_hbm.at[rows] if i == 0 else blocks.at[z, rows], blocks.at[z, rows], block_s.at[k, i], block_r.at[z, i], (d, lax.rem(z + k, Z))
        )

    def own_goes(k):
        t = lax.rem(z + k, Z)
        return jnp.abs(t - z) < 3 if relayed else t >= 0

    def relay_copy(i):
        return block_copy(lax.rem(z + 2, Z), i, 3 * (z - 1), relay_s.at[i])

    middle = (z >= 1) & (z <= 2)

    def tab_copy(k):
        return remote(tables.at[d], tables.at[d], tab_s.at[k], tab_r.at[k], (lax.rem(d + k, n_dp), z))

    def run_copy(k):
        t = lax.rem(d + k, n_dp)
        return remote(run_send.at[t], run_recv.at[d], run_s.at[k], run_r.at[k], (t, z))

    pl.semaphore_wait(barrier, n_dp - 1 + Z - 1)
    def start_own(i):
        for k in sorted(range(1, Z), key=lambda k: abs(k - Z // 2)):

            @pl.when(own_goes(k))
            def _():
                own_copy(k, i).start()

    start_own(0)
    tables[d] = jnp.zeros((8, 128), I32)
    tables[d, 0:1, 0:n_dp] = start_ref[...]
    tables[d, 1:2, 0:n_dp] = length_ref[...]
    tables[d, 2:3, 0:n_dp] = slot_ref[...]
    load.wait()
    weight_load = pltpu.make_async_copy(wqkv_hbm, w_qkv, wload_sem.at[0])
    weight_load.start()
    out_loads = [
        pltpu.make_async_copy(wout_hbm.at[:, pl.ds(m * FL, FL)], w_out.at[m], wload_sem.at[1 + m]) for m in range(Z)
    ]
    for cp in out_loads:
        cp.start()
    x = blocks[z].astype(F32)
    stats[z] = jnp.zeros((8, 128), F32)
    stats[z, 0:1, :] = jnp.broadcast_to(jnp.sum(x, axis=-1, keepdims=True), (T, 128)).T[0:1, :]
    stats[z, 1:2, :] = jnp.broadcast_to(jnp.sum(x * x, axis=-1, keepdims=True), (T, 128)).T[0:1, :]
    for k in range(1, Z):
        stat_copy(k).start()
    for i in range(1, SUB):
        start_own(i)
    for k in range(1, n_dp):
        tab_copy(k).start()

    within = lax.broadcasted_iota(I32, (cap, T), 0)
    lane = lax.broadcasted_iota(I32, (cap, T), 1)
    for p in range(n_dp):
        hit = (within + start_ref[0:1, p : p + 1] == lane) & (within < length_ref[0:1, p : p + 1])
        pick_ref[p * cap : (p + 1) * cap, :] = hit.astype(F32).astype(BF16)
    run_send[...] = (
        jnp.dot(pick_ref[...], blocks[z], preferred_element_type=F32).astype(BF16).reshape(n_dp, cap, FL)
    )
    run_recv[d] = run_send[d]
    for k in range(1, n_dp):
        run_copy(k).start()

    for k in range(1, Z):
        stat_copy(k).wait()
    total = jnp.sum(stats[...], axis=0) * (1.0 / D)
    mean_row = total[0:1, :]
    rstd_row = lax.rsqrt(total[1:2, :] - mean_row * mean_row + epsilon)
    mean_col[...] = jnp.broadcast_to(mean_row, (T, 128)).T
    rstd_col[...] = jnp.broadcast_to(rstd_row, (T, 128)).T

    def norm_copy(m, h, i):
        rows = pl.ds(i * SR, SR)
        return remote(
            normed.at[m, h, rows], gathered.at[d, rows], norm_s.at[m, h, i], norm_r.at[d, i], (2 * m + h, z)
        )

    def spread(m, i):
        rows = pl.ds(i * SR, SR)
        gain = gain_ref[:, pl.ds(pl.multiple_of(m * FL, 128), FL)]
        raw = blocks[m, rows, :].astype(F32)
        done = ((raw - mean_col[rows, 0:1]) * rstd_col[rows, 0:1] * gain).astype(BF16)
        for h in range(2):
            normed[m, h, rows, :] = done[:, h * KS : (h + 1) * KS]

            @pl.when(2 * m + h != d)
            def _():
                norm_copy(m, h, i).start()

            @pl.when(2 * m + h == d)
            def _():
                gathered[d, rows, :] = normed[m, h, rows, :]

    def destinations():
        for k in range(1, n_dp):
            tab_copy(k).wait()
        starts, lengths = tables[:, 0, :], tables[:, 1, :]
        square[...] = jnp.zeros((128, 128), F32)
        square[0:n_dp, :] = tables[:, 2, :].astype(F32)
        slots = square[...].T[0:n_dp, :].astype(I32)
        u = lax.broadcasted_iota(I32, (n_dp, T), 1)
        dest = jnp.zeros((n_dp, T), I32)
        for p in range(n_dp):
            first = starts[:, p : p + 1]
            inside = (u >= first) & (u < first + lengths[:, p : p + 1])
            dest = dest + jnp.where(inside, u + (slots[:, p : p + 1] - first + p * T), 0)
        dest_ref[...] = dest

        same = jnp.broadcast_to(image_ref[...].astype(F32), (T, T))
        mask_ref[...] = (same == same.T).astype(F32)
        k_ref[...] = jnp.zeros_like(k_ref)
        v_ref[...] = jnp.zeros_like(v_ref)

    def place_runs():
        for k in range(1, n_dp):
            run_copy(k).wait()
        spot = lax.broadcasted_iota(I32, (1, n_dp * cap), 1)
        goal = spot % cap
        for s in range(n_dp):
            goal = goal + jnp.where(spot // cap == s, slot_ref[0:1, s : s + 1], 0)
        place_ref[...] = (lax.broadcasted_iota(I32, (T, n_dp * cap), 0) == goal).astype(F32).astype(BF16)
        packed_v[...] = jnp.dot(
            place_ref[...], run_recv[...].reshape(n_dp * cap, FL), preferred_element_type=F32
        ).astype(BF16)
        packed_store.start()

    packed_store = pltpu.make_async_copy(packed_v, packed_hbm, store_sem.at[0])

    def take(m, i):
        block_copy(m, i, z, relay_s.at[i]).wait_recv()

    for i in range(SUB):
        spread(z, i)
        if i == 1:
            destinations()
        if i == 2:
            place_runs()
        for s in [2, 1] + list(range(3, Z)):
            for m in (z - s, z + s):

                @pl.when((m >= 0) & (m < Z))
                def _():
                    take(m, i)

                    if relayed and s == 2:

                        @pl.when(middle)
                        def _():
                            relay_copy(i).start()

                    spread(m, i)

    CR = C * R

    def choose(r):
        row = lax.broadcasted_iota(I32, (2 * CR, T), 0)
        side = row // CR
        row = row % CR
        goal = (row // R) * (2 * T) + row % R + r * R + T * (side * j + (1 - side) * (1 - j))
        for s in range(n_dp):
            chosen[:, s * T : (s + 1) * T] = (dest_ref[s : s + 1, :] == goal).astype(F32).astype(BF16)

    choose(0)

    def wait_gathered(k, i):
        t = lax.rem(d + k, n_dp)
        rows = pl.ds(i * SR, SR)
        remote(normed.at[0, 0, rows], gathered.at[t, rows], norm_s.at[0, 0, i], norm_r.at[t, i], (t, z)).wait_recv()

    for i in range(SUB):

        @pl.loop(1, n_dp)
        def _(k):
            wait_gathered(k, i)

    U = 3 * NCH
    H = NH // 2
    grid = C == 4
    across = c + 1 - 2 * (c % 2), c + 2 - 4 * (c // 2)
    weight_load.wait()

    def pair_copy(u):
        return remote(pair_send.at[u], pair_recv.at[u], pair_s.at[u], pair_r.at[u], sibling)

    def half_copy(u, n):
        return remote(half_send.at[u, n], half_recv.at[u, n], half_s.at[u, n], half_r.at[u, n], (2 * across[n] + j, z))

    def rs_copy(u, n):
        chip = across[n] if grid else lax.rem(c + n + 1, C)
        return remote(rs_send.at[u, n], rs_recv.at[u, n], rs_s.at[u, n], rs_r.at[u, n], (2 * chip + j, z))

    pieces = 2 if grid else C - 1

    def project(u):
        @pl.when(u % 3 == 0)
        def _():
            ordered[...] = jnp.dot(
                chosen[...], gathered[...].reshape(n_dp * T, KS), preferred_element_type=F32
            ).astype(BF16)

        @pl.loop(0, NH // NT)
        def _(n):
            cols = pl.ds(pl.multiple_of(n * NT, 128), NT)
            y = jnp.dot(ordered[...], w_qkv[(u + 1) % 3, :, cols], preferred_element_type=F32)
            pair_send[u, :, cols] = y[:CR].astype(BF16)
            part_own[u % (to_pair + 1), :, cols] = y[CR:]

        pair_copy(u).start()

        @pl.when((u % 3 == 1) & (u < U - 3))
        def _():
            choose(u // 3 + 1)

    def add_pair(u):
        pair_copy(u).wait_recv()

        def total(chip):
            rows = pl.ds(pl.multiple_of(chip * R, R), R)
            return part_own[u % (to_pair + 1), rows, :] + pair_recv[u, rows, :].astype(F32)

        if grid:
            y = total(C - 1 - c)
            for n in range(2):
                half_send[u, n] = y[:, n * H : (n + 1) * H].astype(BF16)
                half_copy(u, n).start()
            for n in range(2):
                held[u % (to_half - to_pair + 1), n] = total(across[n])
        else:
            for n in range(pieces):
                rs_send[u, n] = total(lax.rem(c + n + 1, C)).astype(BF16)
                rs_copy(u, n).start()
        proj_own[u] = total(c)

    def add_half(u):
        if grid:
            for n in range(2):
                half_copy(u, 1 - n).wait_recv()
                near, other = slice((1 - n) * H, (2 - n) * H), slice(n * H, (n + 1) * H)
                rs_send[u, n, :, near] = (held[u % (to_half - to_pair + 1), n, :, near] + half_recv[u, 1 - n].astype(F32)).astype(BF16)
                rs_send[u, n, :, other] = held[u % (to_half - to_pair + 1), n, :, other].astype(BF16)
                rs_copy(u, n).start()

    def receive(u):
        rows = pl.ds(pl.multiple_of((u // 3) * R, R), R)
        for n in range(pieces):
            rs_copy(u, n).wait_recv()
        y = proj_own[u]
        for n in range(pieces):
            y = y + rs_recv[u, n].astype(F32)
        heads = [slice(h * HS, (h + 1) * HS) for h in range(HL)]

        @pl.when(u % 3 == 0)
        def _():
            for cols in heads:
                k_ref[rows, cols] = row_norm(y[:, cols], kgain_ref[...]).astype(BF16)

        @pl.when(u % 3 == 1)
        def _():
            v_ref[rows, :] = y.astype(BF16)

        @pl.when(u % 3 == 2)
        def _():
            for cols in heads:
                q_ref[rows, cols] = row_norm(y[:, cols], qgain_ref[...]).astype(BF16)

    inner = ((z + 1) // 2) % 2
    last = z // 3

    def out_copy(a, k):
        rows = pl.ds(pl.multiple_of(a * R, R), R)
        return remote(
            out_send.at[k, rows], out_recv.at[k, rows], out_s.at[k, a], out_r.at[k, a], (d, lax.rem(z + k, Z))
        )

    def end_copy(a, k):
        rows = pl.ds(pl.multiple_of(a * R, R), R)
        return remote(out_send.at[k, rows], end_recv.at[rows], out_s.at[k, a], end_r.at[a], (d, 1 + last))

    def attend(a):
        rows = pl.ds(pl.multiple_of(a * R, R), R)
        same_image = mask_ref[rows, :] > 0.5
        heads = [slice(h * HS, (h + 1) * HS) for h in range(HL)]
        scores = [
            lax.dot_general(
                q_ref[rows, cols], k_ref[:, cols], (((1,), (1,)), ((), ())), preferred_element_type=F32
            )
            for cols in heads
        ]
        raw = [jnp.where(same_image, jnp.exp(s * HS ** (-0.5)), 0.0) for s in scores]
        totals = [jnp.sum(w, axis=-1, keepdims=True) for w in raw]
        attention = [(w / total).astype(BF16) for w, total in zip(raw, totals)]
        terms = [
            jnp.dot(w, v_ref[:, cols], preferred_element_type=F32).astype(BF16) for w, cols in zip(attention, heads)
        ]
        for term, cols in zip(terms, heads):
            context[:, cols] = term
        for t in range(Z):
            if t == Z - 1:
                k = 0
            elif relayed:
                k = inner * (1, 3, 2)[t] + (1 - inner) * ((1 - last) * (3 - t) + last * (1 + t))
            else:
                k = t + 1
            m = lax.rem(z + k, Z)
            y = jnp.dot(context[...], w_out[m], preferred_element_type=F32).astype(BF16)
            if t == Z - 1:
                out_own[rows, :] = y
            else:
                out_send[k, rows, :] = y
                if not relayed or t == 1:
                    out_copy(a, k).start()
                elif t == 0:

                    @pl.when(inner == 0)
                    def _():
                        end_copy(a, k).start()

                    @pl.when(inner == 1)
                    def _():
                        out_copy(a, k).start()

                else:

                    @pl.when(inner == 0)
                    def _():
                        out_copy(a, k).start()

    def pass_on(a):
        if relayed:

            @pl.when(inner == 1)
            def _():
                rows = pl.ds(pl.multiple_of(a * R, R), R)
                end_copy(a, 2).wait_recv()
                out_send[2, rows, :] = (
                    out_send[2, rows, :].astype(F32) + end_recv[rows, :].astype(F32)
                ).astype(BF16)
                out_copy(a, 2).start()

    for cp in out_loads:
        cp.wait()

    @pl.loop(0, U + to_take)
    def _(v):
        @pl.when(v < U)
        def _():
            project(v)

        @pl.when((v >= to_pair) & (v < U + to_pair))
        def _():
            add_pair(v - to_pair)

        @pl.when((v >= to_half) & (v < U + to_half))
        def _():
            add_half(v - to_half)

        @pl.when(v >= to_take)
        def _():
            u = v - to_take
            receive(u)

            @pl.when((u >= 7) & (u % 3 == 1))
            def _():
                pass_on((u - 7) // 3)

            @pl.when((u >= 4) & (u % 3 == 1))
            def _():
                attend((u - 4) // 3)

    attend(NCH - 1)
    pass_on(NCH - 2)
    pass_on(NCH - 1)

    for i in range(SUB):
        for k in range(1, Z):

            @pl.when(own_goes(k))
            def _():
                own_copy(k, i).wait_send()

        if relayed:

            @pl.when(middle)
            def _():
                relay_copy(i).wait_send()

        for m in range(Z):
            for h in range(2):

                @pl.when(2 * m + h != d)
                def _():
                    norm_copy(m, h, i).wait_send()

    @pl.loop(0, U)
    def _(u):
        pair_copy(u).wait_send()
        for n in range(pieces):
            rs_copy(u, n).wait_send()
        if grid:
            for n in range(2):
                half_copy(u, n).wait_send()

    stores = []
    for a in range(NCH):
        rows = slice(a * R, (a + 1) * R)
        y = out_own[rows, :].astype(F32)
        for k in range(1, Z):
            out_copy(a, k).wait_send()
            if relayed and k != 2:
                direct = jnp.abs(lax.rem(z + Z - k, Z) - z) < 3

                @pl.when(direct)
                def _():
                    out_copy(a, k).wait_recv()

                y = y + jnp.where(direct, out_recv[k, rows, :].astype(F32), 0.0)
            else:
                out_copy(a, k).wait_recv()
                y = y + out_recv[k, rows, :].astype(F32)
        attended_v[rows, :] = y.astype(BF16)
        stores.append(pltpu.make_async_copy(attended_v.at[rows], attended_hbm.at[rows], store_sem.at[1 + a]))
        stores[a].start()
    packed_store.wait()
    for store in stores:
        store.wait()


def hand_over(packed_in, attended_in, packed_out, attended_out, held, load_sem, store_sem):
    piece = held.shape[2]
    loads, stores = [], []
    for n, (source, goal) in enumerate(((packed_in, packed_out), (attended_in, attended_out))):
        for i in range(held.shape[1]):
            rows = pl.ds(i * piece, piece)
            loads.append(pltpu.make_async_copy(source.at[rows], held.at[n, i], load_sem.at[n, i]))
            stores.append(pltpu.make_async_copy(held.at[n, i], goal.at[rows], store_sem.at[n, i]))
    for load in loads:
        load.start()
    for load, store in zip(loads, stores):
        load.wait()
        store.start()
    for store in stores:
        store.wait()


def on_device(
    n_dp, Z, patches, send_start, run_length, slot_start, image_ids, norm_gain, qkv_weight, query_gain, key_gain, out_weight
):
    T, FL = patches.shape
    KS, _, NH = qkv_weight.shape
    HS = query_gain.shape[0]
    C = n_dp // 2
    R, SUB = 32, 4
    NCH = T // R
    U, pieces = 3 * NCH, 2 if C == 4 else C - 1
    cap = max(16, 2 * T // n_dp)
    dims = (n_dp, Z, T, FL, KS, NH, HS, R, SUB, cap)
    dma = pltpu.SemaphoreType.DMA
    vmem = pltpu.VMEM
    scratch = [
        vmem((Z, T, FL), BF16),
        vmem((Z, 2, T, KS), BF16),
        vmem((n_dp, T, KS), BF16),
        vmem((3, KS, NH), BF16),
        vmem((Z, NH, FL), BF16),
        vmem((Z, 8, 128), F32),
        vmem((T, 128), F32),
        vmem((T, 128), F32),
        vmem((128, 128), F32),
        vmem((n_dp, 8, 128), I32),
        vmem((n_dp, T), I32),
        vmem((n_dp * cap, T), BF16),
        vmem((n_dp, cap, FL), BF16),
        vmem((n_dp, cap, FL), BF16),
        vmem((T, n_dp * cap), BF16),
        vmem((T, FL), BF16),
        vmem((2 * C * R, n_dp * T), BF16),
        vmem((2 * C * R, KS), BF16),
        vmem((U, C * R, NH), BF16),
        vmem((U, C * R, NH), BF16),
        vmem((to_pair + 1, C * R, NH), F32),
        vmem((U, 2, R, NH // 2), BF16),
        vmem((U, 2, R, NH // 2), BF16),
        vmem((to_half - to_pair + 1, 2, R, NH), F32),
        vmem((U, pieces, R, NH), BF16),
        vmem((U, pieces, R, NH), BF16),
        vmem((U, R, NH), F32),
        vmem((T, NH), BF16),
        vmem((T, NH), BF16),
        vmem((T, NH), BF16),
        vmem((T, T), F32),
        vmem((R, NH), BF16),
        vmem((Z, T, FL), BF16),
        vmem((Z, T, FL), BF16),
        vmem((T, FL), BF16),
        vmem((T, FL), BF16),
        vmem((T, FL), BF16),
        dma,
        dma((1 + Z,)),
        dma((1 + NCH,)),
        dma((Z,)), dma((Z,)),
        dma((n_dp,)), dma((n_dp,)),
        dma((n_dp,)), dma((n_dp,)),
        dma((Z, SUB)), dma((Z, SUB)), dma((SUB,)),
        dma((Z, 2, SUB)), dma((n_dp, SUB)),
        dma((U,)), dma((U,)),
        dma((U, 2)), dma((U, 2)),
        dma((U, pieces)), dma((U, pieces)),
        dma((Z, NCH)), dma((Z, NCH)), dma((NCH,)),
    ]
    in_vmem = pl.BlockSpec(memory_space=pltpu.VMEM)
    anywhere = pl.BlockSpec(memory_space=pl.ANY)
    outs = pl.pallas_call(
        functools.partial(kernel, dims),
        out_shape=(jax.ShapeDtypeStruct((T, FL), BF16),) * 2,
        in_specs=[anywhere] + [in_vmem] * 5 + [anywhere] + [in_vmem] * 2 + [anywhere],
        out_specs=(anywhere,) * 2,
        scratch_shapes=scratch,
        compiler_params=pltpu.CompilerParams(
            collective_id=0, has_side_effects=True, vmem_limit_bytes=60 * 1024 * 1024
        ),
    )(
        patches, send_start, run_length, slot_start, image_ids, norm_gain.reshape(1, -1),
        jnp.transpose(qkv_weight, (1, 0, 2)), query_gain.reshape(1, -1), key_gain.reshape(1, -1), out_weight,
    )
    return tuple(
        pl.pallas_call(
            hand_over,
            out_shape=(jax.ShapeDtypeStruct((T, FL), BF16),) * 2,
            in_specs=[anywhere] * 2,
            out_specs=(anywhere,) * 2,
            scratch_shapes=[vmem((2, 2, T // 2, FL), BF16), dma((2, 2)), dma((2, 2))],
        )(*outs)
    )


def solution(mesh):
    n_dp, Z = mesh.shape["dp"], mesh.shape["mp"]
    assert n_dp == 2 * Z
    return jax.shard_map(
        functools.partial(on_device, n_dp, Z),
        mesh=mesh,
        in_specs=(
            P("dp", "mp"),
            P("dp", None),
            P("dp", None),
            P("dp", None),
            P("dp", None),
            P(),
            P("dp", None, "mp"),
            P(),
            P(),
            P("mp", None),
        ),
        out_specs=(P("dp", "mp"), P("dp", "mp")),
        check_vma=False,
    )
```
